32 devices in a mesh: maps: 2 (over y), row: 4 (over x, core), col: 4 (over z).
Axes of the slice: x: 2, y: 2, z: 4, core: 2. Of those that a mesh axis runs over, the one named last changes fastest.
Arguments:
- positions: float32 [512, 2, 384], P(('maps', 'row', 'col')), parts along dimension 0, may hold values from 0 to 127
- destination: int32 [512, 1], P(('maps', 'row', 'col')), parts along dimension 0, may hold values from 0 to 15; in each aligned block of 16 rows (0 to 15, 16 to 31, ...) at most 4 rows name the same one
- profile: float32 [65, 65], replicated, may hold values from 0.03 to 1
Outputs:
- magnification: float32 [1024, 512], P(('maps', 'row'), 'col'), parts along dimension 0
The draws below stay inside these ranges and needn't reach their ends.
There are 2 independent parts, one for each index of `maps`. The reference program is written for one: setup_inputs(seed, part) draws one part's arguments, and reference() takes and returns one part's arrays. A program takes and returns all parts, laid end to end along the dimension named above; an argument that names none is the same for every part. Nothing has to cross between parts.
Inputs may be any that keep to these rules, and one draw needn't show every extreme that they name: `destination`: at most 4 of the blocks of one device name one tile.
All inputs are finite; a program needn't handle non-finite values.
Results may differ from the reference program's by a relative error of at most 0.0003.
Values may be sent and summed in bfloat16 or wider, within the bound.
A program may use at most 64 MiB of HBM per device.

```python
import math
import jax
import jax.numpy as jnp
import numpy as np
from jax import lax

TILE = 128
HALO = 32
DISC = 65
MOST = 4
R = 384
TCOLS = 4
TILES = 16
BLK_DEV = 16
BLOCKS = 256
NR = 512
NC = 512


def draw_positions(key, part):
    subkeys = jax.random.split(key, 3)
    low_log = 0.0
    spread = jnp.exp(jax.random.uniform(subkeys[0], (BLOCKS, 1, 1), jnp.float32, low_log, math.log(TILE - 1.0)))
    center = 0.5 * spread + jax.random.uniform(subkeys[1], (BLOCKS, 2, 1), jnp.float32) * (TILE - 1.0 - spread)
    offset = jax.random.uniform(subkeys[2], (BLOCKS, 2, R), jnp.float32) - 0.5
    return jnp.clip(center + spread * offset, 0.0, TILE - 1.0).astype(jnp.float32)


def deal_out(stream_key, own, number, rows, count, top, reach, lean):
    ranking = jax.random.permutation(stream_key, count)
    crowded, ordinary = portions_of(count, rows * top, reach, lean, True), portions_of(count, rows * top, reach, lean, False)
    places = jnp.arange(count)

    def named(lengths, turn):
        used = int((lengths > 0).sum())
        fixed = max(1, used // 4)
        moved = fixed + (places - fixed + turn * (used - fixed)) % max(1, count - fixed)
        return jnp.zeros((count,), jnp.int32).at[ranking[jnp.where(places < fixed, places, moved)]].set(jnp.asarray(lengths, jnp.int32))

    lengths = jnp.where(number % 4 == 0, named(crowded, number // 4), named(ordinary, number - number // 4 - 1))
    mixed = jax.random.permutation(jax.random.fold_in(own, 3), count)
    source_of, sink = mixed[0:count // 2 * 2:2], mixed[1:count // 2 * 2:2]
    slack = jnp.minimum(lengths[source_of] - 1, reach - lengths[sink]) // 2
    slack = jnp.where((source_of == ranking[0]) | (sink == ranking[0]) | (lengths[sink] == 0), 0, jnp.maximum(slack, 0))
    moved = jax.random.randint(jax.random.fold_in(own, 4), (count // 2,), 0, 1 << 20) % (slack + 1)
    lengths = lengths.at[source_of].add(-moved).at[sink].add(moved)
    items = jnp.searchsorted(jnp.cumsum(lengths), jnp.arange(rows * top), side="right").astype(jnp.int32)
    table = items.reshape(top, rows).T
    table = table[jax.random.permutation(jax.random.fold_in(own, 1), rows)]
    turn = jax.random.randint(jax.random.fold_in(own, 2), (rows, 1), 0, top)
    return jnp.take_along_axis(table, (jnp.arange(top)[None, :] + turn) % top, axis=1)


def portions_of(count, total, limit, slope, full):
    weights = [(1 << 20) // math.isqrt(rank ** slope) + 1 for rank in range(1, count + 1)]
    largest = limit if full else min(limit, max(-(-total // count), total * weights[0] // sum(weights)))
    least = 1 if total - largest >= count - 1 else 0
    given, spare = [largest] + [least] * (count - 1), total - largest - least * (count - 1)
    while spare > 0:
        movable = [i for i in range(1, count) if given[i] < largest] or [i for i in range(1, count) if given[i] < limit]
        pool, budget = sum([weights[i] for i in movable]), spare
        for i in movable:
            addition = min(limit - given[i], max(1, budget * weights[i] // pool), spare)
            given[i] = given[i] + addition
            spare = spare - addition
    return np.array(given)


def setup_inputs(seed: int = 0, part: int = 0) -> dict:
    keys = jax.random.split(jax.random.key(seed), 4)
    part_splits = jax.random.split(jax.random.fold_in(keys[3], part), 4)
    positions = draw_positions(jax.random.fold_in(jax.random.fold_in(keys[3], part), 71), part)
    destination_keys = jax.random.split(jax.random.fold_in(part_splits[1], 1), BLOCKS // BLK_DEV)
    destination_turns = jax.random.permutation(jax.random.fold_in(part_splits[1], 3), BLOCKS // BLK_DEV)
    destination = jax.vmap(lambda own, number: deal_out(jax.random.fold_in(part_splits[1], 2), own, number, BLK_DEV, TILES, 1, MOST, 1))(destination_keys, destination_turns).reshape((BLOCKS, 1))
    profile = jnp.clip(jnp.exp(jax.random.uniform(keys[2], (DISC, DISC), jnp.float32, math.log(0.03), math.log(1.0))), 0.03, 1.0)
    return dict(positions=positions, destination=destination, profile=profile)


def to_half(values):
    return lax.optimization_barrier(values.astype(jnp.bfloat16)).astype(jnp.float32)


def reference(positions, destination, profile):
    targets = destination[:, 0].astype(jnp.int32)
    base_row = (targets // TCOLS) * TILE
    base_col = (targets % TCOLS) * TILE
    first = positions[:, 0, :].astype(jnp.float32)
    second = positions[:, 1, :].astype(jnp.float32)
    low_first = jnp.floor(first)
    low_second = jnp.floor(second)
    total = jnp.zeros((NR * NC,), jnp.float32)
    for step_row in (0, 1):
        cell_row = low_first + float(step_row)
        hat_row = to_half(jnp.maximum(0.0, 1.0 - jnp.abs(first - cell_row)))
        row_index = jnp.minimum(cell_row.astype(jnp.int32), TILE - 1)
        row_inside = cell_row < TILE
        for step_col in (0, 1):
            cell_col = low_second + float(step_col)
            hat_col = to_half(jnp.maximum(0.0, 1.0 - jnp.abs(second - cell_col)))
            col_index = jnp.minimum(cell_col.astype(jnp.int32), TILE - 1)
            col_inside = cell_col < TILE
            weight = jnp.where(row_inside & col_inside, hat_row * hat_col, 0.0)
            flat = (base_row[:, None] + row_index) * NC + base_col[:, None] + col_index
            total = total.at[flat.reshape(-1).astype(jnp.int32)].add(weight.reshape(-1))
    source_map = to_half(total.reshape(NR, NC))
    span = jnp.arange(DISC).astype(jnp.float32) - HALO
    inside = (span[:, None] ** 2 + span[None, :] ** 2 <= HALO * HALO).astype(jnp.float32)
    weights = profile * inside
    kernel = to_half(weights / jnp.sum(weights))
    convolved = lax.conv_general_dilated(source_map[None, None], kernel[None, None], (1, 1), ((HALO, HALO), (HALO, HALO)), precision=lax.Precision.HIGHEST)[0, 0]
    return convolved / (BLK_DEV * R / (TILE * TILE))
```

```python
import functools

import jax
import jax.numpy as jnp
from jax import lax
from jax.experimental import pallas as pl
from jax.experimental.pallas import tpu as pltpu
from jax.sharding import PartitionSpec as P

TILE = 128
HALO = 32
MOST = 4
DISC = 2 * HALO + 1
GROUP = 2 * MOST
TOGETHER = 3
BF16 = jnp.bfloat16
F32 = jnp.float32
MESH = pl.DeviceIdType.MESH
SIDES = ((-1, 0), (1, 0), (0, -1), (0, 1), (-1, -1), (-1, 1), (1, -1), (1, 1))


def split3(x):
    high = x.astype(BF16)
    rest = x - high.astype(F32)
    middle = rest.astype(BF16)
    low = (rest - middle.astype(F32)).astype(BF16)
    return high, middle, low


def pack(positions_ref, destination_ref, outgoing):
    blocks = positions_ref.shape[0]
    tiles = outgoing.shape[0]
    targets = destination_ref[...]
    named = lax.broadcasted_iota(jnp.int32, (tiles, blocks), 0) == targets
    onehot = jnp.where(named, 1.0, 0.0)
    earlier = jnp.where(
        lax.broadcasted_iota(jnp.int32, (blocks, blocks), 0)
        < lax.broadcasted_iota(jnp.int32, (blocks, blocks), 1),
        1.0,
        0.0,
    )
    before = jnp.dot(onehot.astype(BF16), earlier.astype(BF16), preferred_element_type=F32)
    rank = jnp.sum(before * onehot, axis=0, keepdims=True).astype(jnp.int32)
    slot = targets * GROUP + rank
    wide = lax.broadcasted_iota(jnp.int32, (tiles * GROUP, blocks), 0)
    first = jnp.where(wide == slot, 1.0, 0.0)
    second = jnp.where(wide == slot + MOST, 1.0, 0.0)
    filled = jnp.sum(first + second, axis=1, keepdims=True)

    def gather(select, coords):
        return sum(
            jnp.dot(select.astype(BF16), part, preferred_element_type=F32) for part in split3(coords)
        )

    picked = gather(first, positions_ref[:, 0, :]) + gather(second, positions_ref[:, 1, :])
    picked = jnp.where(filled > 0.5, picked, -2.0)
    outgoing[...] = picked.reshape(outgoing.shape)


def build_toeplitz(profile_ref, table, toeplitz):
    table[...] = jnp.zeros_like(table)
    weights = profile_ref[...]
    down = lax.broadcasted_iota(jnp.int32, weights.shape, 0) - HALO
    across = lax.broadcasted_iota(jnp.int32, weights.shape, 1) - HALO
    weights = jnp.where(down * down + across * across <= HALO * HALO, weights, 0.0)
    total = jnp.sum(jnp.sum(weights, axis=1, keepdims=True), axis=0, keepdims=True)
    table[0:DISC, 0:DISC] = weights / total
    square = (TILE, TILE)
    row = lax.broadcasted_iota(jnp.int32, square, 0)
    column = lax.broadcasted_iota(jnp.int32, square, 1)
    flip = jnp.where((row + column) % TILE == 0, 1.0, 0.0).astype(BF16)
    table[...] = jnp.dot(table[...].astype(BF16), flip, preferred_element_type=F32)
    core_mask = jnp.abs(row - column) <= HALO
    side_row = row[: 2 * HALO]
    side_mask = jnp.where(side_row < HALO, column[: 2 * HALO], TILE - 1 - column[: 2 * HALO]) < 2 * HALO

    def eight(u, unused):
        v, h = lax.div(u, 2), lax.rem(u, 2)
        lines = table[pl.ds(pl.multiple_of(u * 8, 8), 8), :]
        core = pl.ds(pl.multiple_of(h * TILE, TILE), TILE)
        side = pl.ds(pl.multiple_of(2 * TILE + h * 2 * HALO, 2 * HALO), 2 * HALO)
        for s in range(8):
            line = jnp.broadcast_to(lines[s : s + 1, :], square)
            circulant = pltpu.roll(line, 0, 1, stride=1, stride_axis=0)
            turned = jnp.concatenate([circulant[HALO:], circulant[:HALO]], axis=0)
            columns = slice(s * TILE, (s + 1) * TILE)
            toeplitz[v, core, columns] = jnp.where(core_mask, turned, 0.0).astype(BF16)
            toeplitz[v, side, columns] = jnp.where(side_mask, circulant[: 2 * HALO], 0.0).astype(BF16)
        return unused

    lax.fori_loop(0, 8, eight, 0)


def deposit_group(group, cells, total):
    low = jnp.floor(group)
    here = jnp.maximum(0.0, 1.0 - jnp.abs(group - low))
    there = jnp.maximum(0.0, 1.0 - jnp.abs(group - (low + 1.0)))
    rays = group.shape[1]
    packed = (1, 16, rays)
    zero = jnp.zeros((), BF16)

    def row(x, k):
        return jnp.broadcast_to(x[k : k + 1, :], packed[1:]).astype(BF16).reshape(packed)

    def hat(k):
        base, upper, lower = row(low, k), row(here, k), row(there, k)
        after = row(low + 1.0, k)
        pieces = jnp.where(cells == base, upper, jnp.where(cells == after, lower, zero))
        return pieces.reshape(TILE, rays)

    first = jnp.concatenate([hat(m) for m in range(MOST)], axis=1)
    second = jnp.concatenate([hat(MOST + m) for m in range(MOST)], axis=1)
    return total + lax.dot_general(
        first, second, (((1,), (1,)), ((), ())), preferred_element_type=F32
    )


def body(
    rows,
    cols,
    density,
    positions_hbm,
    destination_hbm,
    profile_hbm,
    out_ref,
    positions_ref,
    destination_ref,
    profile_ref,
    outgoing,
    received,
    table,
    toeplitz,
    centre,
    west,
    east,
    heads,
    tails,
    shifted,
    total,
    send_sems,
    recv_sems,
    halo_send,
    halo_recv,
    load_sems,
):
    tiles = rows * cols
    my_row = lax.axis_index("row")
    my_col = lax.axis_index("col")
    me = my_row * cols + my_col

    loads = [
        pltpu.make_async_copy(source, target, load_sems.at[i])
        for i, (source, target) in enumerate(
            (
                (destination_hbm, destination_ref),
                (positions_hbm, positions_ref),
                (profile_hbm, profile_ref),
            )
        )
    ]
    for load in loads:
        load.start()

    def to_peers(act):
        def along_row(down, unused):
            row = lax.rem(my_row + down, rows)
            for right in range(cols):
                col = lax.rem(my_col + right, cols)
                k = down * cols + right
                if right:
                    act(k, row, col)
                else:

                    @pl.when(down > 0)
                    def _():
                        act(k, row, col)

            return unused

        lax.fori_loop(0, rows, along_row, 0)

    def message(k, row, col):
        return pltpu.make_async_remote_copy(
            src_ref=outgoing.at[row * cols + col],
            dst_ref=received.at[k],
            send_sem=send_sems.at[k],
            recv_sem=recv_sems.at[k],
            device_id={"row": row, "col": col},
            device_id_type=MESH,
        )

    barrier = pltpu.get_barrier_semaphore()

    def greet(k, row, col):
        pl.semaphore_signal(barrier, inc=1, device_id={"row": row, "col": col}, device_id_type=MESH)

    def send(k, row, col):
        message(k, row, col).start()

    to_peers(greet)
    loads[0].wait()
    loads[1].wait()
    pack(positions_ref, destination_ref, outgoing)
    pl.semaphore_wait(barrier, tiles - 1)
    to_peers(send)

    def neighbour(d):
        down, right = SIDES[d]
        return my_row + down, my_col + right

    def present(d):
        row, col = neighbour(d)
        return (row >= 0) & (row < rows) & (col >= 0) & (col < cols)

    top, middle, bottom = slice(0, HALO), slice(HALO, HALO + TILE), slice(HALO + TILE, 2 * HALO + TILE)
    places = (
        centre.at[top],
        centre.at[bottom],
        west.at[1],
        east.at[1],
        west.at[0],
        east.at[0],
        west.at[2],
        east.at[2],
    )
    for d in range(8):

        @pl.when(jnp.logical_not(present(d)))
        def _(d=d):
            places[d][...] = jnp.zeros(places[d].shape, BF16)

    rays = positions_ref.shape[2]
    cell_shape = (TILE // 16, 16, rays)
    cells = (
        lax.broadcasted_iota(jnp.int32, cell_shape, 0) * 16
        + lax.broadcasted_iota(jnp.int32, cell_shape, 1)
    ).astype(F32)
    cells = cells.astype(BF16)
    total[...] = deposit_group(outgoing[me], cells, jnp.zeros((TILE, TILE), F32))

    def take(start, count):
        for i in range(count):
            message(start + i, my_row, my_col).wait_recv()
        partial = total[...]
        for i in range(count):
            partial = deposit_group(received[start + i], cells, partial)
        total[...] = partial

    def together(i, unused):
        take(1 + TOGETHER * i, TOGETHER)
        return unused

    whole, left = divmod(tiles - 1, TOGETHER)
    lax.fori_loop(0, whole, together, 0)
    if left:
        take(1 + TOGETHER * whole, left)

    tile = total[...].astype(BF16)
    centre[middle, :] = tile
    exact = tile.astype(F32)
    quarter = lax.div(lax.broadcasted_iota(jnp.int32, (HALO, TILE), 1), HALO)

    def by_quarter(parts):
        return jnp.where(
            quarter < 2,
            jnp.where(quarter == 0, parts[0], parts[1]),
            jnp.where(quarter == 2, parts[2], parts[3]),
        )

    def turn(x, quarters):
        return pltpu.roll(x, quarters % 4 * HALO, 1) if quarters % 4 else x

    bands = [exact[q * HALO : (q + 1) * HALO] for q in range(4)]
    heads[...] = by_quarter([turn(bands[q], q) for q in range(4)]).astype(BF16)
    tails[...] = by_quarter([turn(bands[q], q - 3) for q in range(4)]).astype(BF16)

    first, last = slice(HALO, 2 * HALO), slice(TILE, HALO + TILE)
    parts = (
        (centre.at[first], centre.at[bottom]),
        (centre.at[last], centre.at[top]),
        (heads, east.at[1]),
        (tails, west.at[1]),
        (heads, east.at[2]),
        (tails, west.at[2]),
        (heads, east.at[0]),
        (tails, west.at[0]),
    )
    opposite = (1, 0, 3, 2, 7, 6, 5, 4)

    def halo(d):
        row, col = neighbour(d)
        return pltpu.make_async_remote_copy(
            src_ref=parts[d][0],
            dst_ref=parts[d][1],
            send_sem=halo_send.at[d],
            recv_sem=halo_recv.at[d],
            device_id={"row": row, "col": col},
            device_id_type=MESH,
        )

    for d in (2, 3, 4, 5, 6, 7, 0, 1):

        @pl.when(present(d))
        def _(d=d):
            halo(d).start()

    loads[2].wait()
    build_toeplitz(profile_ref, table, toeplitz)

    for d in range(8):

        @pl.when(present(opposite[d]))
        def _(d=d):
            halo(d).wait_recv()

    tall = TILE + 2 * HALO
    lanes = lax.broadcasted_iota(jnp.int32, (tall, TILE), 1)
    core = centre[...].astype(F32)
    wests = [west[i].astype(F32) for i in range(3)]
    easts = [east[i].astype(F32) for i in range(3)]

    def band(i, q):
        return by_quarter(
            [turn(wests[i], -q), turn(easts[i], 1 - q), turn(wests[i], 2 - q), turn(easts[i], 3 - q)]
        )

    side = jnp.concatenate([band(0, 3)] + [band(1, q) for q in range(4)] + [band(2, 0)], axis=0)
    spare = jnp.zeros((8, TILE), F32)
    core_later = jnp.concatenate([core[8:], spare], axis=0)
    side_later = jnp.concatenate([side[8:], spare], axis=0)
    sides = jnp.where(lanes < 2 * HALO, side, side_later)
    shifted[:, 0:TILE] = centre[...]
    shifted[:, TILE : 2 * TILE] = core_later.astype(BF16)
    shifted[:, 2 * TILE :] = sides.astype(BF16)

    edge = table[DISC - 1 : DISC, TILE - HALO : TILE - HALO + 1]
    result = core[2 * HALO :] * edge
    for p in range(4):
        columns = slice(2 * p * TILE, 2 * (p + 1) * TILE)
        partial = jnp.zeros((TILE + 16, 2 * TILE), F32)
        for v in range(4):
            partial = partial + jnp.dot(
                shifted[16 * v : 16 * v + TILE + 16, :],
                toeplitz[v, :, columns],
                preferred_element_type=F32,
            )
        result = result + partial[2 * p : 2 * p + TILE, :TILE]
        result = result + partial[2 * p + 1 : 2 * p + 1 + TILE, TILE:]
    out_ref[...] = result * (1.0 / density)

    def drain(k, unused):
        message(k, my_row, my_col).wait_send()
        return unused

    lax.fori_loop(1, tiles, drain, 0)
    for d in range(8):

        @pl.when(present(d))
        def _(d=d):
            halo(d).wait_send()


def shards(positions, destination, profile):
    rows = lax.axis_size("row")
    cols = lax.axis_size("col")
    tiles = rows * cols
    blocks, _, rays = positions.shape
    density = blocks * rays / (TILE * TILE)
    tall = TILE + 2 * HALO
    vmem = pl.BlockSpec(memory_space=pltpu.VMEM)
    return pl.pallas_call(
        functools.partial(body, rows, cols, density),
        out_shape=pltpu.VMEM((TILE, TILE), F32),
        in_specs=[pl.BlockSpec(memory_space=pltpu.HBM)] * 3,
        out_specs=vmem,
        scratch_shapes=[
            pltpu.VMEM((blocks, 2, rays), F32),
            pltpu.VMEM((1, blocks), jnp.int32),
            pltpu.VMEM((DISC, DISC), F32),
            pltpu.VMEM((tiles, GROUP, rays), F32),
            pltpu.VMEM((tiles, GROUP, rays), F32),
            pltpu.VMEM((72, TILE), F32),
            pltpu.VMEM((4, 3 * TILE, 8 * TILE), BF16),
            pltpu.VMEM((tall, TILE), BF16),
            pltpu.VMEM((3, HALO, TILE), BF16),
            pltpu.VMEM((3, HALO, TILE), BF16),
            pltpu.VMEM((HALO, TILE), BF16),
            pltpu.VMEM((HALO, TILE), BF16),
            pltpu.VMEM((tall, 3 * TILE), BF16),
            pltpu.VMEM((TILE, TILE), F32),
            pltpu.SemaphoreType.DMA((tiles,)),
            pltpu.SemaphoreType.DMA((tiles,)),
            pltpu.SemaphoreType.DMA((8,)),
            pltpu.SemaphoreType.DMA((8,)),
            pltpu.SemaphoreType.DMA((3,)),
        ],
        compiler_params=pltpu.CompilerParams(
            collective_id=0, has_side_effects=True
        ),
        name="lens_map",
    )(positions, destination.reshape(1, blocks), profile)


def solution(mesh):
    placed = (P(("maps", "row", "col"), None, None), P(("maps", "row", "col"), None), P())
    return jax.shard_map(
        shards, mesh=mesh, in_specs=placed, out_specs=P(("maps", "row"), "col"), check_vma=False
    )
```

```python
import functools

import jax
import jax.numpy as jnp
from jax import lax
from jax.experimental import pallas as pl
from jax.experimental.pallas import tpu as pltpu
from jax.sharding import PartitionSpec as P

TILE = 128
HALO = 32
MOST = 4
DISC = 2 * HALO + 1
GROUP = 2 * MOST
TOGETHER = 7
FRACTION = 14
BITS = 21
BF16 = jnp.bfloat16
F32 = jnp.float32
MESH = pl.DeviceIdType.MESH
SIDES = ((-1, 0), (1, 0), (0, -1), (0, 1), (-1, -1), (-1, 1), (1, -1), (1, 1))


def code(coords):
    scaled = coords * float(1 << FRACTION)
    whole = jnp.floor(scaled)
    fixed = whole.astype(jnp.int32)
    return jnp.where(scaled > whole, fixed | 1, fixed) + 1


def sevens(x):
    return [((x >> shift) & 127).astype(F32).astype(BF16) for shift in (0, 7, 14)]


def pack(positions_ref, destination_ref, outgoing):
    blocks = positions_ref.shape[0]
    tiles = outgoing.shape[0]
    third = outgoing.shape[2] // 2
    targets = destination_ref[...]
    named = lax.broadcasted_iota(jnp.int32, (tiles, blocks), 0) == targets
    onehot = jnp.where(named, 1.0, 0.0)
    earlier = jnp.where(
        lax.broadcasted_iota(jnp.int32, (blocks, blocks), 0)
        < lax.broadcasted_iota(jnp.int32, (blocks, blocks), 1),
        1.0,
        0.0,
    )
    before = jnp.dot(onehot.astype(BF16), earlier.astype(BF16), preferred_element_type=F32)
    rank = jnp.sum(before * onehot, axis=0, keepdims=True).astype(jnp.int32)
    slot = targets * GROUP + rank
    wide = lax.broadcasted_iota(jnp.int32, (tiles * GROUP, blocks), 0)
    weights = []
    pieces = []
    for c in range(2):
        chosen = jnp.where(wide == slot + c * MOST, 1.0, 0.0)
        weights += [chosen, chosen * 128.0, chosen * 16384.0]
        pieces += sevens(code(positions_ref[:, c, :]))
    picked = jnp.dot(
        jnp.concatenate(weights, axis=1).astype(BF16),
        jnp.concatenate(pieces, axis=0),
        preferred_element_type=F32,
    )
    picked = picked.astype(jnp.int32).reshape(tiles, GROUP, 3 * third)
    low, high, cut = (picked[:, :, i * third : (i + 1) * third] for i in range(3))
    outgoing[:, :, :third] = low | (cut << BITS)
    outgoing[:, :, third:] = high | ((cut >> (32 - BITS)) << BITS)


def unpack(words):
    third = words.shape[1] // 2
    one, two = words[:, :third], words[:, third:]
    mask = (1 << BITS) - 1
    cut = lax.shift_right_logical(one, BITS) | (lax.shift_right_logical(two, BITS) << (32 - BITS))
    return jnp.concatenate([one & mask, two & mask, cut], axis=1)


def build_toeplitz(profile_ref, table, toeplitz):
    table[...] = jnp.zeros_like(table)
    weights = profile_ref[...]
    down = lax.broadcasted_iota(jnp.int32, weights.shape, 0) - HALO
    across = lax.broadcasted_iota(jnp.int32, weights.shape, 1) - HALO
    weights = jnp.where(down * down + across * across <= HALO * HALO, weights, 0.0)
    total = jnp.sum(jnp.sum(weights, axis=1, keepdims=True), axis=0, keepdims=True)
    table[0:DISC, 0:DISC] = weights / total
    square = (TILE, TILE)
    row = lax.broadcasted_iota(jnp.int32, square, 0)
    column = lax.broadcasted_iota(jnp.int32, square, 1)
    flip = jnp.where((row + column) % TILE == 0, 1.0, 0.0).astype(BF16)
    table[...] = jnp.dot(table[...].astype(BF16), flip, preferred_element_type=F32)
    core_mask = jnp.abs(row - column) <= HALO
    side_row = row[: 2 * HALO]
    side_mask = jnp.where(side_row < HALO, column[: 2 * HALO], TILE - 1 - column[: 2 * HALO]) < 2 * HALO

    def eight(u, unused):
        v, h = lax.div(u, 2), lax.rem(u, 2)
        lines = table[pl.ds(pl.multiple_of(u * 8, 8), 8), :]
        core = pl.ds(pl.multiple_of(h * TILE, TILE), TILE)
        side = pl.ds(pl.multiple_of(2 * TILE + h * 2 * HALO, 2 * HALO), 2 * HALO)
        for s in range(8):
            line = jnp.broadcast_to(lines[s : s + 1, :], square)
            circulant = pltpu.roll(line, 0, 1, stride=1, stride_axis=0)
            turned = jnp.concatenate([circulant[HALO:], circulant[:HALO]], axis=0)
            columns = slice(s * TILE, (s + 1) * TILE)
            toeplitz[v, core, columns] = jnp.where(core_mask, turned, 0.0).astype(BF16)
            toeplitz[v, side, columns] = jnp.where(side_mask, circulant[: 2 * HALO], 0.0).astype(BF16)
        return unused

    lax.fori_loop(0, 8, eight, 0)


def deposit_group(group, cells, total):
    fixed = unpack(group)
    filled = fixed > 0
    fixed = fixed - 1
    low = (fixed >> FRACTION).astype(F32)
    part = (fixed & ((1 << FRACTION) - 1)).astype(F32) * (1.0 / (1 << FRACTION))
    here = 1.0 - part
    there = jnp.where(filled, part, 0.0)
    rays = fixed.shape[1]
    packed = (1, 16, rays)
    zero = jnp.zeros((), BF16)

    def row(x, k):
        return jnp.broadcast_to(x[k : k + 1, :], packed[1:]).astype(BF16).reshape(packed)

    def hat(k):
        base, upper, lower = row(low, k), row(here, k), row(there, k)
        after = row(low + 1.0, k)
        pieces = jnp.where(cells == base, upper, jnp.where(cells == after, lower, zero))
        return pieces.reshape(TILE, rays)

    first = jnp.concatenate([hat(m) for m in range(MOST)], axis=1)
    second = jnp.concatenate([hat(MOST + m) for m in range(MOST)], axis=1)
    return total + lax.dot_general(
        first, second, (((1,), (1,)), ((), ())), preferred_element_type=F32
    )


def body(
    rows,
    cols,
    density,
    positions_hbm,
    destination_hbm,
    profile_hbm,
    out_ref,
    positions_ref,
    destination_ref,
    profile_ref,
    outgoing,
    received,
    table,
    toeplitz,
    centre,
    west,
    east,
    heads,
    tails,
    shifted,
    total,
    send_sems,
    recv_sems,
    notices,
    halo_send,
    halo_recv,
    load_sems,
):
    tiles = rows * cols
    my_row = lax.axis_index("row")
    my_col = lax.axis_index("col")
    me = my_row * cols + my_col
    mine = my_col * rows + my_row

    loads = [
        pltpu.make_async_copy(source, target, load_sems.at[i])
        for i, (source, target) in enumerate(
            (
                (destination_hbm, destination_ref),
                (positions_hbm, positions_ref),
                (profile_hbm, profile_ref),
            )
        )
    ]
    for load in loads:
        load.start()

    def device(order):
        return {"row": lax.rem(order, rows), "col": lax.div(order, rows)}

    def message(source, target):
        at = device(target)
        return pltpu.make_async_remote_copy(
            src_ref=outgoing.at[at["row"] * cols + at["col"]],
            dst_ref=received.at[source],
            send_sem=send_sems.at[target],
            recv_sem=recv_sems.at[source],
            device_id=at,
            device_id_type=MESH,
        )

    barrier = pltpu.get_barrier_semaphore()

    def greet(target, unused):
        pl.semaphore_signal(barrier, inc=1, device_id=device(target), device_id_type=MESH)
        return unused

    lax.fori_loop(mine + 1, tiles, greet, 0)

    def settle(semaphore, count):
        @pl.when(count > 0)
        def _():
            pl.semaphore_wait(semaphore, count)

    settle(barrier, mine)
    near = rows * (2 if cols % 2 == 0 else 1)
    base = lax.div(mine, near) * near
    edge_top = base + near

    def tell_near(target, unused):
        pl.semaphore_signal(notices.at[0], inc=1, device_id=device(target), device_id_type=MESH)
        return unused

    def tell_far(target, unused):
        pl.semaphore_signal(notices.at[1], inc=1, device_id=device(target), device_id_type=MESH)
        return unused

    lax.fori_loop(base, mine, tell_near, 0)
    lax.fori_loop(0, base, tell_far, 0)
    loads[0].wait()
    loads[1].wait()
    pack(positions_ref, destination_ref, outgoing)

    def send(target, unused):
        message(mine, target).start()
        return unused

    lax.fori_loop(0, mine, send, 0)
    settle(notices.at[0], edge_top - 1 - mine)
    lax.fori_loop(mine + 1, edge_top, send, 0)
    loads[2].wait()
    build_toeplitz(profile_ref, table, toeplitz)
    settle(notices.at[1], tiles - edge_top)
    lax.fori_loop(edge_top, tiles, send, 0)

    def partner(j):
        ahead = mine + j
        within = jnp.where(ahead >= edge_top, ahead - near, ahead)
        rest = j - near
        return jnp.where(j < near, within, jnp.where(rest < base, rest, rest + near))

    def neighbour(d):
        down, right = SIDES[d]
        return my_row + down, my_col + right

    def present(d):
        row, col = neighbour(d)
        return (row >= 0) & (row < rows) & (col >= 0) & (col < cols)

    top, middle, bottom = slice(0, HALO), slice(HALO, HALO + TILE), slice(HALO + TILE, 2 * HALO + TILE)
    places = (
        centre.at[top],
        centre.at[bottom],
        west.at[1],
        east.at[1],
        west.at[0],
        east.at[0],
        west.at[2],
        east.at[2],
    )
    for d in range(8):

        @pl.when(jnp.logical_not(present(d)))
        def _(d=d):
            places[d][...] = jnp.zeros(places[d].shape, BF16)

    rays = positions_ref.shape[2]
    cell_shape = (TILE // 16, 16, rays)
    cells = (
        lax.broadcasted_iota(jnp.int32, cell_shape, 0) * 16
        + lax.broadcasted_iota(jnp.int32, cell_shape, 1)
    ).astype(F32)
    cells = cells.astype(BF16)
    total[...] = deposit_group(outgoing[me], cells, jnp.zeros((TILE, TILE), F32))

    def take(start, count):
        sources = [partner(start + i) for i in range(count)]
        for source in sources:
            message(source, mine).wait_recv()
        partial = total[...]
        for source in sources:
            partial = deposit_group(received[source], cells, partial)
        total[...] = partial

    def together(i, unused):
        take(1 + TOGETHER * i, TOGETHER)
        return unused

    whole = (tiles - 2) // TOGETHER
    lax.fori_loop(0, whole, together, 0)
    for j in range(1 + TOGETHER * whole, tiles):
        take(j, 1)

    tile = total[...].astype(BF16)
    centre[middle, :] = tile
    exact = tile.astype(F32)
    quarter = lax.div(lax.broadcasted_iota(jnp.int32, (HALO, TILE), 1), HALO)

    def by_quarter(parts):
        return jnp.where(
            quarter < 2,
            jnp.where(quarter == 0, parts[0], parts[1]),
            jnp.where(quarter == 2, parts[2], parts[3]),
        )

    def turn(x, quarters):
        return pltpu.roll(x, quarters % 4 * HALO, 1) if quarters % 4 else x

    bands = [exact[q * HALO : (q + 1) * HALO] for q in range(4)]
    heads[...] = by_quarter([turn(bands[q], q) for q in range(4)]).astype(BF16)
    tails[...] = by_quarter([turn(bands[q], q - 3) for q in range(4)]).astype(BF16)

    first, last = slice(HALO, 2 * HALO), slice(TILE, HALO + TILE)
    parts = (
        (centre.at[first], centre.at[bottom]),
        (centre.at[last], centre.at[top]),
        (heads, east.at[1]),
        (tails, west.at[1]),
        (heads, east.at[2]),
        (tails, west.at[2]),
        (heads, east.at[0]),
        (tails, west.at[0]),
    )
    opposite = (1, 0, 3, 2, 7, 6, 5, 4)

    def halo(d):
        row, col = neighbour(d)
        return pltpu.make_async_remote_copy(
            src_ref=parts[d][0],
            dst_ref=parts[d][1],
            send_sem=halo_send.at[d],
            recv_sem=halo_recv.at[d],
            device_id={"row": row, "col": col},
            device_id_type=MESH,
        )

    for d in (2, 3, 4, 5, 6, 7, 0, 1):

        @pl.when(present(d))
        def _(d=d):
            halo(d).start()

    for d in range(8):

        @pl.when(present(opposite[d]))
        def _(d=d):
            halo(d).wait_recv()

    tall = TILE + 2 * HALO
    lanes = lax.broadcasted_iota(jnp.int32, (tall, TILE), 1)
    core = centre[...].astype(F32)
    wests = [west[i].astype(F32) for i in range(3)]
    easts = [east[i].astype(F32) for i in range(3)]

    def band(i, q):
        return by_quarter(
            [turn(wests[i], -q), turn(easts[i], 1 - q), turn(wests[i], 2 - q), turn(easts[i], 3 - q)]
        )

    side = jnp.concatenate([band(0, 3)] + [band(1, q) for q in range(4)] + [band(2, 0)], axis=0)
    spare = jnp.zeros((8, TILE), F32)
    core_later = jnp.concatenate([core[8:], spare], axis=0)
    side_later = jnp.concatenate([side[8:], spare], axis=0)
    sides = jnp.where(lanes < 2 * HALO, side, side_later)
    shifted[:, 0:TILE] = centre[...]
    shifted[:, TILE : 2 * TILE] = core_later.astype(BF16)
    shifted[:, 2 * TILE :] = sides.astype(BF16)

    edge = table[DISC - 1 : DISC, TILE - HALO : TILE - HALO + 1]
    result = core[2 * HALO :] * edge
    for p in range(4):
        columns = slice(2 * p * TILE, 2 * (p + 1) * TILE)
        partial = jnp.zeros((TILE + 16, 2 * TILE), F32)
        for v in range(4):
            partial = partial + jnp.dot(
                shifted[16 * v : 16 * v + TILE + 16, :],
                toeplitz[v, :, columns],
                preferred_element_type=F32,
            )
        result = result + partial[2 * p : 2 * p + TILE, :TILE]
        result = result + partial[2 * p + 1 : 2 * p + 1 + TILE, TILE:]
    out_ref[...] = result * (1.0 / density)

    def drain(target, unused):
        @pl.when(target != mine)
        def _():
            message(mine, target).wait_send()

        return unused

    lax.fori_loop(0, tiles, drain, 0)
    for d in range(8):

        @pl.when(present(d))
        def _(d=d):
            halo(d).wait_send()


def shards(positions, destination, profile):
    rows = lax.axis_size("row")
    cols = lax.axis_size("col")
    tiles = rows * cols
    blocks, _, rays = positions.shape
    density = blocks * rays / (TILE * TILE)
    tall = TILE + 2 * HALO
    vmem = pl.BlockSpec(memory_space=pltpu.VMEM)
    return pl.pallas_call(
        functools.partial(body, rows, cols, density),
        out_shape=pltpu.VMEM((TILE, TILE), F32),
        in_specs=[pl.BlockSpec(memory_space=pltpu.HBM)] * 3,
        out_specs=vmem,
        scratch_shapes=[
            pltpu.VMEM((blocks, 2, rays), F32),
            pltpu.VMEM((1, blocks), jnp.int32),
            pltpu.VMEM((DISC, DISC), F32),
            pltpu.VMEM((tiles, GROUP, 2 * rays // 3), jnp.int32),
            pltpu.VMEM((tiles, GROUP, 2 * rays // 3), jnp.int32),
            pltpu.VMEM((72, TILE), F32),
            pltpu.VMEM((4, 3 * TILE, 8 * TILE), BF16),
            pltpu.VMEM((tall, TILE), BF16),
            pltpu.VMEM((3, HALO, TILE), BF16),
            pltpu.VMEM((3, HALO, TILE), BF16),
            pltpu.VMEM((HALO, TILE), BF16),
            pltpu.VMEM((HALO, TILE), BF16),
            pltpu.VMEM((tall, 3 * TILE), BF16),
            pltpu.VMEM((TILE, TILE), F32),
            pltpu.SemaphoreType.DMA((tiles,)),
            pltpu.SemaphoreType.DMA((tiles,)),
            pltpu.SemaphoreType.REGULAR((2,)),
            pltpu.SemaphoreType.DMA((8,)),
            pltpu.SemaphoreType.DMA((8,)),
            pltpu.SemaphoreType.DMA((3,)),
        ],
        compiler_params=pltpu.CompilerParams(
            collective_id=0, has_side_effects=True
        ),
        name="lens_map",
    )(positions, destination.reshape(1, blocks), profile)


def solution(mesh):
    placed = (P(("maps", "row", "col"), None, None), P(("maps", "row", "col"), None), P())
    return jax.shard_map(
        shards, mesh=mesh, in_specs=placed, out_specs=P(("maps", "row"), "col"), check_vma=False
    )
```

```python
import functools

import jax
import jax.numpy as jnp
from jax import lax
from jax.experimental import pallas as pl
from jax.experimental.pallas import tpu as pltpu
from jax.sharding import PartitionSpec as P

TILE = 128
HALO = 32
MOST = 4
DISC = 2 * HALO + 1
GROUP = 2 * MOST
TOGETHER = 8
FRACTION = 14
BITS = 21
BF16 = jnp.bfloat16
F32 = jnp.float32
MESH = pl.DeviceIdType.MESH
SIDES = ((-1, 0), (1, 0), (0, -1), (0, 1), (-1, -1), (-1, 1), (1, -1), (1, 1))


def code(coords):
    scaled = coords * float(1 << FRACTION)
    whole = jnp.floor(scaled)
    fixed = whole.astype(jnp.int32)
    return jnp.where(scaled > whole, fixed | 1, fixed) + 1


def sevens(x):
    return [((x >> shift) & 127).astype(F32).astype(BF16) for shift in (0, 7, 14)]


def choose(destination_ref, tiles):
    blocks = destination_ref.shape[1]
    wide = 6 * blocks
    targets = jnp.concatenate([destination_ref[...]] * 6, axis=1)
    lane = lax.broadcasted_iota(jnp.int32, (1, wide), 1)
    piece = sum((lane >= i * blocks).astype(jnp.int32) for i in range(1, 6))
    onehot = jnp.where(lax.broadcasted_iota(jnp.int32, (tiles, wide), 0) == targets, 1.0, 0.0)
    earlier = jnp.where(
        lax.broadcasted_iota(jnp.int32, (blocks, wide), 0) < lane - piece * blocks, 1.0, 0.0
    )
    before = jnp.dot(
        onehot[:, :blocks].astype(BF16), earlier.astype(BF16), preferred_element_type=F32
    )
    rank = jnp.sum(before * onehot, axis=0, keepdims=True).astype(jnp.int32)
    second = piece >= 3
    slot = targets * GROUP + rank + jnp.where(second, MOST, 0)
    order = jnp.where(second, piece - 3, piece)
    weight = jnp.where(order == 0, 1.0, jnp.where(order == 1, 128.0, 16384.0))
    rows = lax.broadcasted_iota(jnp.int32, (tiles * GROUP, wide), 0)
    return jnp.where(rows == slot, weight, 0.0).astype(BF16)


def pack(positions_ref, chosen, outgoing):
    tiles = outgoing.shape[0]
    third = outgoing.shape[2] // 2
    pieces = [piece for c in range(2) for piece in sevens(code(positions_ref[:, c, :]))]
    picked = jnp.dot(chosen, jnp.concatenate(pieces, axis=0), preferred_element_type=F32)
    picked = picked.astype(jnp.int32).reshape(tiles, GROUP, 3 * third)
    low, high, cut = (picked[:, :, i * third : (i + 1) * third] for i in range(3))
    outgoing[:, :, :third] = low | (cut << BITS)
    outgoing[:, :, third:] = high | ((cut >> (32 - BITS)) << BITS)


def unpack(words):
    third = words.shape[1] // 2
    one, two = words[:, :third], words[:, third:]
    mask = (1 << BITS) - 1
    cut = lax.shift_right_logical(one, BITS) | (lax.shift_right_logical(two, BITS) << (32 - BITS))
    return jnp.concatenate([one & mask, two & mask, cut], axis=1)


def build_toeplitz(profile_ref, table, inner, outer):
    table[...] = jnp.zeros_like(table)
    weights = profile_ref[...]
    down = lax.broadcasted_iota(jnp.int32, weights.shape, 0) - HALO
    across = lax.broadcasted_iota(jnp.int32, weights.shape, 1) - HALO
    weights = jnp.where(down * down + across * across <= HALO * HALO, weights, 0.0)
    total = jnp.sum(jnp.sum(weights, axis=1, keepdims=True), axis=0, keepdims=True)
    table[0:DISC, 0:DISC] = weights / total
    square = (TILE, TILE)
    row = lax.broadcasted_iota(jnp.int32, square, 0)
    column = lax.broadcasted_iota(jnp.int32, square, 1)
    flip = jnp.where((row + column) % TILE == 0, 1.0, 0.0).astype(BF16)
    table[...] = jnp.dot(table[...].astype(BF16), flip, preferred_element_type=F32)
    core_mask = jnp.abs(row - column) <= HALO
    side_row = row[: 2 * HALO]
    side_mask = jnp.where(side_row < HALO, column[: 2 * HALO], TILE - 1 - column[: 2 * HALO]) < 2 * HALO

    def eight(u, unused):
        v, h = lax.div(u, 2), lax.rem(u, 2)
        lines = table[pl.ds(pl.multiple_of(u * 8, 8), 8), :]
        core = pl.ds(pl.multiple_of(h * TILE, TILE), TILE)
        side = pl.ds(pl.multiple_of(lax.rem(u, 4) * 2 * HALO, 2 * HALO), 2 * HALO)
        for s in range(8):
            line = jnp.broadcast_to(lines[s : s + 1, :], square)
            circulant = pltpu.roll(line, 0, 1, stride=1, stride_axis=0)
            turned = jnp.concatenate([circulant[HALO:], circulant[:HALO]], axis=0)
            columns = slice(s * TILE, (s + 1) * TILE)
            inner[v, core, columns] = jnp.where(core_mask, turned, 0.0).astype(BF16)
            outer[lax.div(u, 4), side, columns] = jnp.where(side_mask, circulant[: 2 * HALO], 0.0).astype(BF16)
        return unused

    lax.fori_loop(0, 8, eight, 0)


def deposit_group(group, cells, total):
    fixed = unpack(group)
    filled = fixed > 0
    fixed = fixed - 1
    low = (fixed >> FRACTION).astype(F32)
    part = (fixed & ((1 << FRACTION) - 1)).astype(F32) * (1.0 / (1 << FRACTION))
    here = 1.0 - part
    there = jnp.where(filled, part, 0.0)
    rays = fixed.shape[1]
    packed = (1, 16, rays)
    zero = jnp.zeros((), BF16)

    def row(x, k):
        return jnp.broadcast_to(x[k : k + 1, :], packed[1:]).astype(BF16).reshape(packed)

    def hat(k):
        base, upper, lower = row(low, k), row(here, k), row(there, k)
        after = row(low + 1.0, k)
        pieces = jnp.where(cells == base, upper, jnp.where(cells == after, lower, zero))
        return pieces.reshape(TILE, rays)

    first = jnp.concatenate([hat(m) for m in range(MOST)], axis=1)
    second = jnp.concatenate([hat(MOST + m) for m in range(MOST)], axis=1)
    return total + lax.dot_general(
        first, second, (((1,), (1,)), ((), ())), preferred_element_type=F32
    )


def body(
    rows,
    cols,
    density,
    positions_hbm,
    destination_hbm,
    profile_hbm,
    out_ref,
    positions_ref,
    destination_ref,
    profile_ref,
    outgoing,
    received,
    table,
    inner,
    outer,
    tile_ref,
    north,
    south,
    west,
    east,
    heads,
    tails,
    shifted,
    beside,
    own,
    total,
    send_sems,
    recv_sems,
    notices,
    halo_send,
    halo_recv,
    load_sems,
):
    tiles = rows * cols
    my_row = lax.axis_index("row")
    my_col = lax.axis_index("col")
    me = my_row * cols + my_col
    mine = my_col * rows + my_row

    loads = [
        pltpu.make_async_copy(source, target, load_sems.at[i])
        for i, (source, target) in enumerate(
            (
                (destination_hbm, destination_ref),
                (positions_hbm, positions_ref),
                (profile_hbm, profile_ref),
            )
        )
    ]
    for load in loads:
        load.start()

    def device(order):
        return {"row": lax.rem(order, rows), "col": lax.div(order, rows)}

    def message(source, target):
        at = device(target)
        return pltpu.make_async_remote_copy(
            src_ref=outgoing.at[at["row"] * cols + at["col"]],
            dst_ref=received.at[source],
            send_sem=send_sems.at[target],
            recv_sem=recv_sems.at[source],
            device_id=at,
            device_id_type=MESH,
        )

    barrier = pltpu.get_barrier_semaphore()

    def greet(target, unused):
        pl.semaphore_signal(barrier, inc=1, device_id=device(target), device_id_type=MESH)
        return unused

    lax.fori_loop(mine + 1, tiles, greet, 0)

    def settle(semaphore, count):
        @pl.when(count > 0)
        def _():
            pl.semaphore_wait(semaphore, count)

    settle(barrier, mine)

    def tell(target, unused):
        pl.semaphore_signal(
            notices.at[my_col], inc=1, device_id=device(target), device_id_type=MESH
        )
        return unused

    lax.fori_loop(0, mine, lambda i, u: tell(mine - 1 - i, u), 0)
    loads[0].wait()
    chosen = choose(destination_ref, tiles)
    loads[1].wait()
    pack(positions_ref, chosen, outgoing)

    def send(target, unused):
        message(mine, target).start()
        return unused

    lax.fori_loop(0, mine, send, 0)

    def send_up(col, unused):
        first = jnp.maximum(col * rows, mine + 1)
        settle(notices.at[col], (col + 1) * rows - first)
        lax.fori_loop(first, (col + 1) * rows, send, 0)

        @pl.when(col == jnp.minimum(my_col + 1, cols - 1))
        def _():
            loads[2].wait()
            build_toeplitz(profile_ref, table, inner, outer)

        return unused

    lax.fori_loop(my_col, cols, send_up, 0)
    near = rows * (2 if cols % 2 == 0 else 1)
    base = lax.div(mine, near) * near
    ceiling = base + near

    def partner(j):
        ahead = mine + j
        within = jnp.where(ahead >= ceiling, ahead - near, ahead)
        rest = j - near
        return jnp.where(j < near, within, jnp.where(rest < base, rest, rest + near))

    def neighbour(d):
        down, right = SIDES[d]
        return my_row + down, my_col + right

    def present(d):
        row, col = neighbour(d)
        return (row >= 0) & (row < rows) & (col >= 0) & (col < cols)

    places = (
        north,
        south,
        west.at[1],
        east.at[1],
        west.at[0],
        east.at[0],
        west.at[2],
        east.at[2],
    )
    for d in range(8):

        @pl.when(jnp.logical_not(present(d)))
        def _(d=d):
            places[d][...] = jnp.zeros(places[d].shape, BF16)

    rays = positions_ref.shape[2]
    cell_shape = (TILE // 16, 16, rays)
    cells = (
        lax.broadcasted_iota(jnp.int32, cell_shape, 0) * 16
        + lax.broadcasted_iota(jnp.int32, cell_shape, 1)
    ).astype(F32)
    cells = cells.astype(BF16)
    received[mine] = outgoing[me]
    total[...] = jnp.zeros((TILE, TILE), F32)

    def take(i, unused):
        sources = [partner(TOGETHER * i + j) for j in range(TOGETHER)]
        for source in sources:

            @pl.when(source != mine)
            def _(source=source):
                message(source, mine).wait_recv()

        partial = total[...]
        for source in sources:
            partial = deposit_group(received[source], cells, partial)
        total[...] = partial
        return unused

    lax.fori_loop(0, tiles // TOGETHER, take, 0)

    tile = total[...].astype(BF16)
    tile_ref[...] = tile
    exact = tile.astype(F32)
    quarter = lax.div(lax.broadcasted_iota(jnp.int32, (HALO, TILE), 1), HALO)

    def by_quarter(parts):
        return jnp.where(
            quarter < 2,
            jnp.where(quarter == 0, parts[0], parts[1]),
            jnp.where(quarter == 2, parts[2], parts[3]),
        )

    def turn(x, quarters):
        return pltpu.roll(x, quarters % 4 * HALO, 1) if quarters % 4 else x

    bands = [exact[q * HALO : (q + 1) * HALO] for q in range(4)]
    heads[...] = by_quarter([turn(bands[q], q) for q in range(4)]).astype(BF16)
    tails[...] = by_quarter([turn(bands[q], q - 3) for q in range(4)]).astype(BF16)

    first, last = slice(0, HALO), slice(TILE - HALO, TILE)
    parts = (
        (tile_ref.at[first], south),
        (tile_ref.at[last], north),
        (heads, east.at[1]),
        (tails, west.at[1]),
        (heads, east.at[2]),
        (tails, west.at[2]),
        (heads, east.at[0]),
        (tails, west.at[0]),
    )
    opposite = (1, 0, 3, 2, 7, 6, 5, 4)

    def halo(d):
        row, col = neighbour(d)
        return pltpu.make_async_remote_copy(
            src_ref=parts[d][0],
            dst_ref=parts[d][1],
            send_sem=halo_send.at[d],
            recv_sem=halo_recv.at[d],
            device_id={"row": row, "col": col},
            device_id_type=MESH,
        )

    for d in (2, 3, 4, 5, 6, 7, 0, 1):

        @pl.when(present(d))
        def _(d=d):
            halo(d).start()

    def empty(lines):
        return jnp.zeros((lines, TILE), F32)

    def sweep(products):
        def step(i, sums):
            product = products(pl.ds(pl.multiple_of((3 - i) * 2 * TILE, 2 * TILE), 2 * TILE))
            tall = product.shape[0]
            odd = pltpu.roll(product[:, TILE:], tall - 1, 0)
            return pltpu.roll(sums, tall - 2, 0) + product[:, :TILE] + odd

        return lax.fori_loop(0, 4, step, jnp.zeros((TILE + 16, TILE), F32), unroll=True)[:TILE]

    def dot(a, b):
        return jnp.dot(a, b, preferred_element_type=F32)

    shifted[:, :TILE] = jnp.concatenate([empty(HALO), exact, empty(HALO)], axis=0).astype(BF16)
    shifted[:, TILE:] = jnp.concatenate(
        [empty(HALO - 8), exact, empty(HALO + 8)], axis=0
    ).astype(BF16)
    own[...] = sweep(
        lambda columns: sum(
            dot(shifted[16 * v : 16 * v + TILE + 16, :], inner[v, :, columns]) for v in range(4)
        )
    )

    for d in range(8):

        @pl.when(present(opposite[d]))
        def _(d=d):
            halo(d).wait_recv()

    tall = TILE + 2 * HALO
    lanes = lax.broadcasted_iota(jnp.int32, (tall, TILE), 1)
    wests = [west[i].astype(F32) for i in range(3)]
    easts = [east[i].astype(F32) for i in range(3)]

    def band(i, q):
        return by_quarter(
            [turn(wests[i], -q), turn(easts[i], 1 - q), turn(wests[i], 2 - q), turn(easts[i], 3 - q)]
        )

    side = jnp.concatenate([band(0, 3)] + [band(1, q) for q in range(4)] + [band(2, 0)], axis=0)
    side_later = jnp.concatenate([side[8:], empty(8)], axis=0)
    sides = jnp.where(lanes < 2 * HALO, side, side_later).astype(BF16)
    beside[:, :TILE] = sides[: tall - 16]
    beside[:, TILE:] = sides[16:]
    above = north[...].astype(F32)
    below = south[...].astype(F32)
    before = jnp.concatenate(
        [above, jnp.concatenate([above[8:], empty(8)], axis=0)], axis=1
    ).astype(BF16)
    after = jnp.concatenate(
        [jnp.concatenate([empty(8), below[:-8]], axis=0), below], axis=1
    ).astype(BF16)

    def around(columns):
        wide = sum(
            dot(beside[32 * v : 32 * v + TILE + 16, :], outer[v, :, columns]) for v in range(2)
        )
        upper = dot(before, inner[0, :, columns])
        upper_next = dot(before[16:], inner[1, :, columns])
        lower = dot(after, inner[3, :, columns])
        lower_next = dot(after[:16], inner[2, :, columns])
        end = TILE + 8 - HALO
        return jnp.concatenate(
            [
                wide[:16] + upper[:16] + upper_next,
                wide[16:HALO] + upper[16:],
                wide[HALO:end],
                wide[end : end + 16] + lower[:16],
                wide[end + 16 : end + 32] + lower[16:] + lower_next,
                wide[end + 32 :],
            ],
            axis=0,
        )

    edge = table[DISC - 1 : DISC, TILE - HALO : TILE - HALO + 1]
    result = own[...] + jnp.concatenate([exact[HALO:], below], axis=0) * edge + sweep(around)
    out_ref[...] = result * (1.0 / density)

    def drain(target, unused):
        @pl.when(target != mine)
        def _():
            message(mine, target).wait_send()

        return unused

    lax.fori_loop(0, tiles, drain, 0)
    for d in range(8):

        @pl.when(present(d))
        def _(d=d):
            halo(d).wait_send()


def shards(positions, destination, profile):
    rows = lax.axis_size("row")
    cols = lax.axis_size("col")
    tiles = rows * cols
    blocks, _, rays = positions.shape
    density = blocks * rays / (TILE * TILE)
    tall = TILE + 2 * HALO
    vmem = pl.BlockSpec(memory_space=pltpu.VMEM)
    return pl.pallas_call(
        functools.partial(body, rows, cols, density),
        out_shape=pltpu.VMEM((TILE, TILE), F32),
        in_specs=[pl.BlockSpec(memory_space=pltpu.HBM)] * 3,
        out_specs=vmem,
        scratch_shapes=[
            pltpu.VMEM((blocks, 2, rays), F32),
            pltpu.VMEM((1, blocks), jnp.int32),
            pltpu.VMEM((DISC, DISC), F32),
            pltpu.VMEM((tiles, GROUP, 2 * rays // 3), jnp.int32),
            pltpu.VMEM((tiles, GROUP, 2 * rays // 3), jnp.int32),
            pltpu.VMEM((72, TILE), F32),
            pltpu.VMEM((4, 2 * TILE, 8 * TILE), BF16),
            pltpu.VMEM((2, 2 * TILE, 8 * TILE), BF16),
            pltpu.VMEM((TILE, TILE), BF16),
            pltpu.VMEM((HALO, TILE), BF16),
            pltpu.VMEM((HALO, TILE), BF16),
            pltpu.VMEM((3, HALO, TILE), BF16),
            pltpu.VMEM((3, HALO, TILE), BF16),
            pltpu.VMEM((HALO, TILE), BF16),
            pltpu.VMEM((HALO, TILE), BF16),
            pltpu.VMEM((tall, 2 * TILE), BF16),
            pltpu.VMEM((tall - 16, 2 * TILE), BF16),
            pltpu.VMEM((TILE, TILE), F32),
            pltpu.VMEM((TILE, TILE), F32),
            pltpu.SemaphoreType.DMA((tiles,)),
            pltpu.SemaphoreType.DMA((tiles,)),
            pltpu.SemaphoreType.REGULAR((cols,)),
            pltpu.SemaphoreType.DMA((8,)),
            pltpu.SemaphoreType.DMA((8,)),
            pltpu.SemaphoreType.DMA((3,)),
        ],
        compiler_params=pltpu.CompilerParams(
            collective_id=0, has_side_effects=True
        ),
        name="lens_map",
    )(positions, destination.reshape(1, blocks), profile)


def solution(mesh):
    placed = (P(("maps", "row", "col"), None, None), P(("maps", "row", "col"), None), P())
    return jax.shard_map(
        shards, mesh=mesh, in_specs=placed, out_specs=P(("maps", "row"), "col"), check_vma=False
    )
```

```python
import functools

import jax
import jax.numpy as jnp
from jax import lax
from jax.experimental import pallas as pl
from jax.experimental.pallas import tpu as pltpu
from jax.sharding import PartitionSpec as P

TILE = 128
HALO = 32
MOST = 4
DISC = 2 * HALO + 1
GROUP = 2 * MOST
TOGETHER = 8
FRACTION = 14
BITS = 21
BF16 = jnp.bfloat16
F32 = jnp.float32
MESH = pl.DeviceIdType.MESH
SIDES = ((-1, 0), (1, 0), (0, -1), (0, 1), (-1, -1), (-1, 1), (1, -1), (1, 1))


def code(coords):
    scaled = coords * float(1 << FRACTION)
    whole = jnp.floor(scaled)
    fixed = whole.astype(jnp.int32)
    return jnp.where(scaled > whole, fixed | 1, fixed) + 1


def sevens(x):
    return [((x >> shift) & 127).astype(F32).astype(BF16) for shift in (0, 7, 14)]


def choose(destination_ref, tiles):
    blocks = destination_ref.shape[1]
    wide = 6 * blocks
    targets = jnp.concatenate([destination_ref[...]] * 6, axis=1)
    lane = lax.broadcasted_iota(jnp.int32, (1, wide), 1)
    piece = sum((lane >= i * blocks).astype(jnp.int32) for i in range(1, 6))
    onehot = jnp.where(lax.broadcasted_iota(jnp.int32, (tiles, wide), 0) == targets, 1.0, 0.0)
    earlier = jnp.where(
        lax.broadcasted_iota(jnp.int32, (blocks, wide), 0) < lane - piece * blocks, 1.0, 0.0
    )
    before = jnp.dot(
        onehot[:, :blocks].astype(BF16), earlier.astype(BF16), preferred_element_type=F32
    )
    rank = jnp.sum(before * onehot, axis=0, keepdims=True).astype(jnp.int32)
    second = piece >= 3
    slot = targets * GROUP + rank + jnp.where(second, MOST, 0)
    order = jnp.where(second, piece - 3, piece)
    weight = jnp.where(order == 0, 1.0, jnp.where(order == 1, 128.0, 16384.0))
    rows = lax.broadcasted_iota(jnp.int32, (tiles * GROUP, wide), 0)
    return jnp.where(rows == slot, weight, 0.0).astype(BF16)


def pack(positions_ref, chosen, outgoing):
    tiles = outgoing.shape[0]
    third = outgoing.shape[2] // 2
    pieces = [piece for c in range(2) for piece in sevens(code(positions_ref[:, c, :]))]
    picked = jnp.dot(chosen, jnp.concatenate(pieces, axis=0), preferred_element_type=F32)
    picked = picked.astype(jnp.int32).reshape(tiles, GROUP, 3 * third)
    low, high, cut = (picked[:, :, i * third : (i + 1) * third] for i in range(3))
    outgoing[:, :, :third] = low | (cut << BITS)
    outgoing[:, :, third:] = high | ((cut >> (32 - BITS)) << BITS)


def unpack(words):
    third = words.shape[1] // 2
    one, two = words[:, :third], words[:, third:]
    mask = (1 << BITS) - 1
    cut = lax.shift_right_logical(one, BITS) | (lax.shift_right_logical(two, BITS) << (32 - BITS))
    return jnp.concatenate([one & mask, two & mask, cut], axis=1)


def build_toeplitz(profile_ref, table, inner, outer):
    table[...] = jnp.zeros_like(table)
    weights = profile_ref[...]
    down = lax.broadcasted_iota(jnp.int32, weights.shape, 0) - HALO
    across = lax.broadcasted_iota(jnp.int32, weights.shape, 1) - HALO
    weights = jnp.where(down * down + across * across <= HALO * HALO, weights, 0.0)
    total = jnp.sum(jnp.sum(weights, axis=1, keepdims=True), axis=0, keepdims=True)
    table[0:DISC, 0:DISC] = weights / total
    square = (TILE, TILE)
    row = lax.broadcasted_iota(jnp.int32, square, 0)
    column = lax.broadcasted_iota(jnp.int32, square, 1)
    flip = jnp.where((row + column) % TILE == 0, 1.0, 0.0).astype(BF16)
    table[...] = jnp.dot(table[...].astype(BF16), flip, preferred_element_type=F32)
    core_mask = jnp.abs(row - column) <= HALO
    side_row = row[: 2 * HALO]
    side_mask = jnp.where(side_row < HALO, column[: 2 * HALO], TILE - 1 - column[: 2 * HALO]) < 2 * HALO

    def eight(u, unused):
        v, h = lax.div(u, 2), lax.rem(u, 2)
        lines = table[pl.ds(pl.multiple_of(u * 8, 8), 8), :]
        core = pl.ds(pl.multiple_of(h * TILE, TILE), TILE)
        side = pl.ds(pl.multiple_of(lax.rem(u, 4) * 2 * HALO, 2 * HALO), 2 * HALO)
        for s in range(8):
            line = jnp.broadcast_to(lines[s : s + 1, :], square)
            circulant = pltpu.roll(line, 0, 1, stride=1, stride_axis=0)
            turned = jnp.concatenate([circulant[HALO:], circulant[:HALO]], axis=0)
            columns = slice(s * TILE, (s + 1) * TILE)
            inner[v, core, columns] = jnp.where(core_mask, turned, 0.0).astype(BF16)
            outer[lax.div(u, 4), side, columns] = jnp.where(side_mask, circulant[: 2 * HALO], 0.0).astype(BF16)
        return unused

    lax.fori_loop(0, 8, eight, 0)


def deposit_group(group, cells, total):
    fixed = unpack(group)
    filled = fixed > 0
    fixed = fixed - 1
    low = (fixed >> FRACTION).astype(F32)
    part = (fixed & ((1 << FRACTION) - 1)).astype(F32) * (1.0 / (1 << FRACTION))
    here = 1.0 - part
    there = jnp.where(filled, part, 0.0)
    rays = fixed.shape[1]
    packed = (1, 16, rays)
    zero = jnp.zeros((), BF16)

    def row(x, k):
        return jnp.broadcast_to(x[k : k + 1, :], packed[1:]).astype(BF16).reshape(packed)

    def hat(k):
        base, upper, lower = row(low, k), row(here, k), row(there, k)
        after = row(low + 1.0, k)
        pieces = jnp.where(cells == base, upper, jnp.where(cells == after, lower, zero))
        return pieces.reshape(TILE, rays)

    first = jnp.concatenate([hat(m) for m in range(MOST)], axis=1)
    second = jnp.concatenate([hat(MOST + m) for m in range(MOST)], axis=1)
    return total + lax.dot_general(
        first, second, (((1,), (1,)), ((), ())), preferred_element_type=F32
    )


def body(
    rows,
    cols,
    density,
    positions_hbm,
    destination_hbm,
    profile_hbm,
    out_ref,
    positions_ref,
    destination_ref,
    profile_ref,
    outgoing,
    received,
    table,
    inner,
    outer,
    tile_ref,
    north,
    south,
    west,
    east,
    heads,
    tails,
    shifted,
    beside,
    own,
    total,
    send_sems,
    recv_sems,
    notices,
    halo_send,
    halo_recv,
    load_sems,
):
    tiles = rows * cols
    my_row = lax.axis_index("row")
    my_col = lax.axis_index("col")
    me = my_row * cols + my_col
    mine = my_col * rows + my_row

    loads = [
        pltpu.make_async_copy(source, target, load_sems.at[i])
        for i, (source, target) in enumerate(
            (
                (destination_hbm, destination_ref),
                (positions_hbm, positions_ref),
                (profile_hbm, profile_ref),
            )
        )
    ]
    for load in loads:
        load.start()

    def message(source, at):
        target = at["col"] * rows + at["row"]
        return pltpu.make_async_remote_copy(
            src_ref=outgoing.at[at["row"] * cols + at["col"]],
            dst_ref=received.at[source],
            send_sem=send_sems.at[target],
            recv_sem=recv_sems.at[source],
            device_id=at,
            device_id_type=MESH,
        )

    here = {"row": my_row, "col": my_col}

    def device(order):
        return {"row": lax.rem(order, rows), "col": lax.div(order, rows)}

    barrier = pltpu.get_barrier_semaphore()

    def greet(target, unused):
        pl.semaphore_signal(barrier, inc=1, device_id=device(target), device_id_type=MESH)
        return unused

    lax.fori_loop(mine + 1, tiles, greet, 0)

    def settle(semaphore, count):
        @pl.when(count > 0)
        def _():
            pl.semaphore_wait(semaphore, count)

    settle(barrier, mine)

    def tell(at):
        pl.semaphore_signal(notices.at[my_col], inc=1, device_id=at, device_id_type=MESH)

    def lower(act):
        def column(col, unused):
            for row in reversed(range(rows)):
                act({"row": row, "col": col})
            return unused

        def inside(row, unused):
            act({"row": row, "col": my_col})
            return unused

        lax.fori_loop(0, my_col, column, 0)
        lax.fori_loop(0, my_row, inside, 0)

    lower(tell)
    loads[0].wait()
    chosen = choose(destination_ref, tiles)
    loads[1].wait()
    pack(positions_ref, chosen, outgoing)

    def start(at):
        message(mine, at).start()

    lower(start)

    def send_up(col, unused):
        first = jnp.where(col == my_col, my_row + 1, 0)
        settle(notices.at[col], rows - first)

        def each(row, done):
            start({"row": row, "col": col})
            return done

        lax.fori_loop(first, rows, each, 0)

        return unused

    lax.fori_loop(my_col, cols, send_up, 0)
    near = rows * (2 if cols % 2 == 0 else 1)
    base = lax.div(mine, near) * near
    ceiling = base + near

    def partner(j):
        ahead = mine + j
        within = jnp.where(ahead >= ceiling, ahead - near, ahead)
        rest = j - near
        return jnp.where(j < near, within, jnp.where(rest < base, rest, rest + near))

    def neighbour(d):
        down, right = SIDES[d]
        return my_row + down, my_col + right

    def present(d):
        row, col = neighbour(d)
        return (row >= 0) & (row < rows) & (col >= 0) & (col < cols)

    places = (
        north,
        south,
        west.at[1],
        east.at[1],
        west.at[0],
        east.at[0],
        west.at[2],
        east.at[2],
    )
    for d in range(8):

        @pl.when(jnp.logical_not(present(d)))
        def _(d=d):
            places[d][...] = jnp.zeros(places[d].shape, BF16)

    rays = positions_ref.shape[2]
    cell_shape = (TILE // 16, 16, rays)
    cells = (
        lax.broadcasted_iota(jnp.int32, cell_shape, 0) * 16
        + lax.broadcasted_iota(jnp.int32, cell_shape, 1)
    ).astype(F32)
    cells = cells.astype(BF16)
    received[mine] = outgoing[me]
    total[...] = jnp.zeros((TILE, TILE), F32)

    def take(i, unused):
        sources = [partner(TOGETHER * i + j) for j in range(TOGETHER)]
        for source in sources:

            @pl.when(source != mine)
            def _(source=source):
                message(source, here).wait_recv()

        partial = total[...]
        for source in sources:
            partial = deposit_group(received[source], cells, partial)
        total[...] = partial
        return unused

    lax.fori_loop(0, tiles // TOGETHER, take, 0)

    tile = total[...].astype(BF16)
    tile_ref[...] = tile
    exact = tile.astype(F32)
    quarter = lax.div(lax.broadcasted_iota(jnp.int32, (HALO, TILE), 1), HALO)

    def by_quarter(parts):
        return jnp.where(
            quarter < 2,
            jnp.where(quarter == 0, parts[0], parts[1]),
            jnp.where(quarter == 2, parts[2], parts[3]),
        )

    def turn(x, quarters):
        return pltpu.roll(x, quarters % 4 * HALO, 1) if quarters % 4 else x

    bands = [exact[q * HALO : (q + 1) * HALO] for q in range(4)]
    heads[...] = by_quarter([turn(bands[q], q) for q in range(4)]).astype(BF16)
    tails[...] = by_quarter([turn(bands[q], q - 3) for q in range(4)]).astype(BF16)

    first, last = slice(0, HALO), slice(TILE - HALO, TILE)
    parts = (
        (tile_ref.at[first], south),
        (tile_ref.at[last], north),
        (heads, east.at[1]),
        (tails, west.at[1]),
        (heads, east.at[2]),
        (tails, west.at[2]),
        (heads, east.at[0]),
        (tails, west.at[0]),
    )
    opposite = (1, 0, 3, 2, 7, 6, 5, 4)

    def halo(d):
        row, col = neighbour(d)
        return pltpu.make_async_remote_copy(
            src_ref=parts[d][0],
            dst_ref=parts[d][1],
            send_sem=halo_send.at[d],
            recv_sem=halo_recv.at[d],
            device_id={"row": row, "col": col},
            device_id_type=MESH,
        )

    for d in (2, 3, 4, 5, 6, 7, 0, 1):

        @pl.when(present(d))
        def _(d=d):
            halo(d).start()

    loads[2].wait()
    build_toeplitz(profile_ref, table, inner, outer)

    def empty(lines):
        return jnp.zeros((lines, TILE), F32)

    def sweep(products):
        def step(i, sums):
            product = products(pl.ds(pl.multiple_of((3 - i) * 2 * TILE, 2 * TILE), 2 * TILE))
            tall = product.shape[0]
            odd = pltpu.roll(product[:, TILE:], tall - 1, 0)
            return pltpu.roll(sums, tall - 2, 0) + product[:, :TILE] + odd

        return lax.fori_loop(0, 4, step, jnp.zeros((TILE + 16, TILE), F32), unroll=True)[:TILE]

    def dot(a, b):
        return jnp.dot(a, b, preferred_element_type=F32)

    shifted[:, :TILE] = jnp.concatenate([empty(HALO), exact, empty(HALO)], axis=0).astype(BF16)
    shifted[:, TILE:] = jnp.concatenate(
        [empty(HALO - 8), exact, empty(HALO + 8)], axis=0
    ).astype(BF16)
    own[...] = sweep(
        lambda columns: sum(
            dot(shifted[16 * v : 16 * v + TILE + 16, :], inner[v, :, columns]) for v in range(4)
        )
    )

    for d in range(8):

        @pl.when(present(opposite[d]))
        def _(d=d):
            halo(d).wait_recv()

    tall = TILE + 2 * HALO
    lanes = lax.broadcasted_iota(jnp.int32, (tall, TILE), 1)
    wests = [west[i].astype(F32) for i in range(3)]
    easts = [east[i].astype(F32) for i in range(3)]

    def band(i, q):
        return by_quarter(
            [turn(wests[i], -q), turn(easts[i], 1 - q), turn(wests[i], 2 - q), turn(easts[i], 3 - q)]
        )

    side = jnp.concatenate([band(0, 3)] + [band(1, q) for q in range(4)] + [band(2, 0)], axis=0)
    side_later = jnp.concatenate([side[8:], empty(8)], axis=0)
    sides = jnp.where(lanes < 2 * HALO, side, side_later).astype(BF16)
    beside[:, :TILE] = sides[: tall - 16]
    beside[:, TILE:] = sides[16:]
    above = north[...].astype(F32)
    below = south[...].astype(F32)
    before = jnp.concatenate(
        [above, jnp.concatenate([above[8:], empty(8)], axis=0)], axis=1
    ).astype(BF16)
    after = jnp.concatenate(
        [jnp.concatenate([empty(8), below[:-8]], axis=0), below], axis=1
    ).astype(BF16)

    def around(columns):
        wide = sum(
            dot(beside[32 * v : 32 * v + TILE + 16, :], outer[v, :, columns]) for v in range(2)
        )
        upper = dot(before, inner[0, :, columns])
        upper_next = dot(before[16:], inner[1, :, columns])
        lower = dot(after, inner[3, :, columns])
        lower_next = dot(after[:16], inner[2, :, columns])
        end = TILE + 8 - HALO
        return jnp.concatenate(
            [
                wide[:16] + upper[:16] + upper_next,
                wide[16:HALO] + upper[16:],
                wide[HALO:end],
                wide[end : end + 16] + lower[:16],
                wide[end + 16 : end + 32] + lower[16:] + lower_next,
                wide[end + 32 :],
            ],
            axis=0,
        )

    edge = table[DISC - 1 : DISC, TILE - HALO : TILE - HALO + 1]
    result = own[...] + jnp.concatenate([exact[HALO:], below], axis=0) * edge + sweep(around)
    out_ref[...] = result * (1.0 / density)

    def drain(target, unused):
        @pl.when(target != mine)
        def _():
            message(mine, device(target)).wait_send()

        return unused

    lax.fori_loop(0, tiles, drain, 0)
    for d in range(8):

        @pl.when(present(d))
        def _(d=d):
            halo(d).wait_send()


def shards(positions, destination, profile):
    rows = lax.axis_size("row")
    cols = lax.axis_size("col")
    tiles = rows * cols
    blocks, _, rays = positions.shape
    density = blocks * rays / (TILE * TILE)
    tall = TILE + 2 * HALO
    vmem = pl.BlockSpec(memory_space=pltpu.VMEM)
    return pl.pallas_call(
        functools.partial(body, rows, cols, density),
        out_shape=pltpu.VMEM((TILE, TILE), F32),
        in_specs=[pl.BlockSpec(memory_space=pltpu.HBM)] * 3,
        out_specs=vmem,
        scratch_shapes=[
            pltpu.VMEM((blocks, 2, rays), F32),
            pltpu.VMEM((1, blocks), jnp.int32),
            pltpu.VMEM((DISC, DISC), F32),
            pltpu.VMEM((tiles, GROUP, 2 * rays // 3), jnp.int32),
            pltpu.VMEM((tiles, GROUP, 2 * rays // 3), jnp.int32),
            pltpu.VMEM((72, TILE), F32),
            pltpu.VMEM((4, 2 * TILE, 8 * TILE), BF16),
            pltpu.VMEM((2, 2 * TILE, 8 * TILE), BF16),
            pltpu.VMEM((TILE, TILE), BF16),
            pltpu.VMEM((HALO, TILE), BF16),
            pltpu.VMEM((HALO, TILE), BF16),
            pltpu.VMEM((3, HALO, TILE), BF16),
            pltpu.VMEM((3, HALO, TILE), BF16),
            pltpu.VMEM((HALO, TILE), BF16),
            pltpu.VMEM((HALO, TILE), BF16),
            pltpu.VMEM((tall, 2 * TILE), BF16),
            pltpu.VMEM((tall - 16, 2 * TILE), BF16),
            pltpu.VMEM((TILE, TILE), F32),
            pltpu.VMEM((TILE, TILE), F32),
            pltpu.SemaphoreType.DMA((tiles,)),
            pltpu.SemaphoreType.DMA((tiles,)),
            pltpu.SemaphoreType.REGULAR((cols,)),
            pltpu.SemaphoreType.DMA((8,)),
            pltpu.SemaphoreType.DMA((8,)),
            pltpu.SemaphoreType.DMA((3,)),
        ],
        compiler_params=pltpu.CompilerParams(
            collective_id=0, has_side_effects=True
        ),
        name="lens_map",
    )(positions, destination.reshape(1, blocks), profile)


def solution(mesh):
    placed = (P(("maps", "row", "col"), None, None), P(("maps", "row", "col"), None), P())
    return jax.shard_map(
        shards, mesh=mesh, in_specs=placed, out_specs=P(("maps", "row"), "col"), check_vma=False
    )
```

```python
import functools

import jax
import jax.numpy as jnp
from jax import lax
from jax.experimental import pallas as pl
from jax.experimental.pallas import tpu as pltpu
from jax.sharding import PartitionSpec as P

TILE = 128
HALO = 32
MOST = 4
DISC = 2 * HALO + 1
GROUP = 2 * MOST
TOGETHER = 8
FRACTION = 14
BITS = 21
BF16 = jnp.bfloat16
F32 = jnp.float32
MESH = pl.DeviceIdType.MESH
SIDES = ((-1, 0), (1, 0), (0, -1), (0, 1), (-1, -1), (-1, 1), (1, -1), (1, 1))


def code(coords):
    scaled = coords * float(1 << FRACTION)
    whole = jnp.floor(scaled)
    fixed = whole.astype(jnp.int32)
    return jnp.where(scaled > whole, fixed | 1, fixed) + 1


def sevens(x):
    return [((x >> shift) & 127).astype(F32).astype(BF16) for shift in (0, 7, 14)]


def choose(destination_ref, tiles):
    blocks = destination_ref.shape[1]
    wide = 6 * blocks
    targets = jnp.concatenate([destination_ref[...]] * 6, axis=1)
    lane = lax.broadcasted_iota(jnp.int32, (1, wide), 1)
    piece = sum((lane >= i * blocks).astype(jnp.int32) for i in range(1, 6))
    onehot = jnp.where(lax.broadcasted_iota(jnp.int32, (tiles, wide), 0) == targets, 1.0, 0.0)
    earlier = jnp.where(
        lax.broadcasted_iota(jnp.int32, (blocks, wide), 0) < lane - piece * blocks, 1.0, 0.0
    )
    before = jnp.dot(
        onehot[:, :blocks].astype(BF16), earlier.astype(BF16), preferred_element_type=F32
    )
    rank = jnp.sum(before * onehot, axis=0, keepdims=True).astype(jnp.int32)
    second = piece >= 3
    slot = targets * GROUP + rank + jnp.where(second, MOST, 0)
    order = jnp.where(second, piece - 3, piece)
    weight = jnp.where(order == 0, 1.0, jnp.where(order == 1, 128.0, 16384.0))
    rows = lax.broadcasted_iota(jnp.int32, (tiles * GROUP, wide), 0)
    return jnp.where(rows == slot, weight, 0.0).astype(BF16)


def pack(positions_ref, chosen, outgoing):
    tiles = outgoing.shape[0]
    third = outgoing.shape[2] // 2
    pieces = [piece for c in range(2) for piece in sevens(code(positions_ref[:, c, :]))]
    picked = jnp.dot(chosen, jnp.concatenate(pieces, axis=0), preferred_element_type=F32)
    picked = picked.astype(jnp.int32).reshape(tiles, GROUP, 3 * third)
    low, high, cut = (picked[:, :, i * third : (i + 1) * third] for i in range(3))
    outgoing[:, :, :third] = low | (cut << BITS)
    outgoing[:, :, third:] = high | ((cut >> (32 - BITS)) << BITS)


def unpack(words):
    third = words.shape[1] // 2
    one, two = words[:, :third], words[:, third:]
    mask = (1 << BITS) - 1
    cut = lax.shift_right_logical(one, BITS) | (lax.shift_right_logical(two, BITS) << (32 - BITS))
    return jnp.concatenate([one & mask, two & mask, cut], axis=1)


def build_toeplitz(profile_ref, table, inner, outer):
    table[...] = jnp.zeros_like(table)
    weights = profile_ref[...]
    down = lax.broadcasted_iota(jnp.int32, weights.shape, 0) - HALO
    across = lax.broadcasted_iota(jnp.int32, weights.shape, 1) - HALO
    weights = jnp.where(down * down + across * across <= HALO * HALO, weights, 0.0)
    total = jnp.sum(jnp.sum(weights, axis=1, keepdims=True), axis=0, keepdims=True)
    table[0:DISC, 0:DISC] = weights / total
    square = (TILE, TILE)
    row = lax.broadcasted_iota(jnp.int32, square, 0)
    column = lax.broadcasted_iota(jnp.int32, square, 1)
    flip = jnp.where((row + column) % TILE == 0, 1.0, 0.0).astype(BF16)
    table[...] = jnp.dot(table[...].astype(BF16), flip, preferred_element_type=F32)
    core_mask = jnp.abs(row - column) <= HALO
    side_row = row[: 2 * HALO]
    side_mask = jnp.where(side_row < HALO, column[: 2 * HALO], TILE - 1 - column[: 2 * HALO]) < 2 * HALO

    def eight(u, unused):
        v, h = lax.div(u, 2), lax.rem(u, 2)
        lines = table[pl.ds(pl.multiple_of(u * 8, 8), 8), :]
        core = pl.ds(pl.multiple_of(h * TILE, TILE), TILE)
        side = pl.ds(pl.multiple_of(lax.rem(u, 4) * 2 * HALO, 2 * HALO), 2 * HALO)
        for s in range(8):
            line = jnp.broadcast_to(lines[s : s + 1, :], square)
            circulant = pltpu.roll(line, 0, 1, stride=1, stride_axis=0)
            turned = jnp.concatenate([circulant[HALO:], circulant[:HALO]], axis=0)
            columns = slice(s * TILE, (s + 1) * TILE)
            inner[v, core, columns] = jnp.where(core_mask, turned, 0.0).astype(BF16)
            outer[lax.div(u, 4), side, columns] = jnp.where(side_mask, circulant[: 2 * HALO], 0.0).astype(BF16)
        return unused

    lax.fori_loop(0, 8, eight, 0)


def deposit_group(group, cells, total):
    fixed = unpack(group)
    filled = fixed > 0
    fixed = fixed - 1
    part = (fixed & ((1 << FRACTION) - 1)).astype(F32) * (1.0 / (1 << FRACTION))
    low = (fixed >> FRACTION).astype(F32).astype(BF16)
    here = (1.0 - part).astype(BF16)
    there = jnp.where(filled, part, 0.0).astype(BF16)
    rays = fixed.shape[1]
    packed = (1, 16, rays)
    zero = jnp.zeros((), BF16)
    earlier = cells - jnp.ones((), BF16)

    def row(x, k):
        return jnp.broadcast_to(x[k : k + 1, :], packed[1:]).reshape(packed)

    def hat(k):
        base, upper, lower = row(low, k), row(here, k), row(there, k)
        pieces = jnp.where(cells == base, upper, jnp.where(earlier == base, lower, zero))
        return pieces.reshape(TILE, rays)

    first = jnp.concatenate([hat(m) for m in range(MOST)], axis=1)
    second = jnp.concatenate([hat(MOST + m) for m in range(MOST)], axis=1)
    return total + lax.dot_general(
        first, second, (((1,), (1,)), ((), ())), preferred_element_type=F32
    )


def body(
    rows,
    cols,
    density,
    positions_hbm,
    destination_hbm,
    profile_hbm,
    out_ref,
    positions_ref,
    destination_ref,
    profile_ref,
    outgoing,
    received,
    table,
    inner,
    outer,
    tile_ref,
    north,
    south,
    west,
    east,
    heads,
    tails,
    shifted,
    beside,
    own,
    total,
    send_sems,
    recv_sems,
    notices,
    halo_send,
    halo_recv,
    load_sems,
):
    tiles = rows * cols
    my_row = lax.axis_index("row")
    my_col = lax.axis_index("col")
    me = my_row * cols + my_col
    mine = my_col * rows + my_row

    loads = [
        pltpu.make_async_copy(source, target, load_sems.at[i])
        for i, (source, target) in enumerate(
            (
                (destination_hbm, destination_ref),
                (positions_hbm, positions_ref),
                (profile_hbm, profile_ref),
            )
        )
    ]
    for load in loads:
        load.start()

    def message(source, at):
        target = at["col"] * rows + at["row"]
        return pltpu.make_async_remote_copy(
            src_ref=outgoing.at[at["row"] * cols + at["col"]],
            dst_ref=received.at[source],
            send_sem=send_sems.at[target],
            recv_sem=recv_sems.at[source],
            device_id=at,
            device_id_type=MESH,
        )

    here = {"row": my_row, "col": my_col}

    def device(order):
        return {"row": lax.rem(order, rows), "col": lax.div(order, rows)}

    barrier = pltpu.get_barrier_semaphore()

    def greet(target, unused):
        pl.semaphore_signal(barrier, inc=1, device_id=device(target), device_id_type=MESH)
        return unused

    lax.fori_loop(mine + 1, tiles, greet, 0)

    def settle(semaphore, count):
        @pl.when(count > 0)
        def _():
            pl.semaphore_wait(semaphore, count)

    settle(barrier, mine)

    def tell(at):
        pl.semaphore_signal(notices.at[my_col], inc=1, device_id=at, device_id_type=MESH)

    def lower(act):
        def column(col, unused):
            for row in reversed(range(rows)):
                act({"row": row, "col": col})
            return unused

        def inside(row, unused):
            act({"row": row, "col": my_col})
            return unused

        lax.fori_loop(0, my_col, column, 0)
        lax.fori_loop(0, my_row, inside, 0)

    lower(tell)
    loads[0].wait()
    chosen = choose(destination_ref, tiles)
    loads[1].wait()
    pack(positions_ref, chosen, outgoing)

    def start(at):
        message(mine, at).start()

    lower(start)

    def send_up(col, unused):
        first = jnp.where(col == my_col, my_row + 1, 0)
        settle(notices.at[col], rows - first)

        def each(row, done):
            start({"row": row, "col": col})
            return done

        lax.fori_loop(first, rows, each, 0)

        return unused

    lax.fori_loop(my_col, cols, send_up, 0)
    near = rows * (2 if cols % 2 == 0 else 1)
    base = lax.div(mine, near) * near
    ceiling = base + near

    def partner(j):
        ahead = mine + j
        within = jnp.where(ahead >= ceiling, ahead - near, ahead)
        rest = j - near
        return jnp.where(j < near, within, jnp.where(rest < base, base - 1 - rest, j))

    def neighbour(d):
        down, right = SIDES[d]
        return my_row + down, my_col + right

    def present(d):
        row, col = neighbour(d)
        return (row >= 0) & (row < rows) & (col >= 0) & (col < cols)

    places = (
        north,
        south,
        west.at[1],
        east.at[1],
        west.at[0],
        east.at[0],
        west.at[2],
        east.at[2],
    )
    for d in range(8):

        @pl.when(jnp.logical_not(present(d)))
        def _(d=d):
            places[d][...] = jnp.zeros(places[d].shape, BF16)

    rays = positions_ref.shape[2]
    cell_shape = (TILE // 16, 16, rays)
    cells = (
        lax.broadcasted_iota(jnp.int32, cell_shape, 0) * 16
        + lax.broadcasted_iota(jnp.int32, cell_shape, 1)
    ).astype(F32)
    cells = cells.astype(BF16)
    received[mine] = outgoing[me]
    total[...] = jnp.zeros((TILE, TILE), F32)

    def take(i, unused):
        sources = [partner(TOGETHER * i + j) for j in range(TOGETHER)]
        for source in sources:

            @pl.when(source != mine)
            def _(source=source):
                message(source, here).wait_recv()

        partial = total[...]
        for source in sources:
            partial = deposit_group(received[source], cells, partial)
        total[...] = partial
        return unused

    lax.fori_loop(0, tiles // TOGETHER, take, 0)

    tile = total[...].astype(BF16)
    tile_ref[...] = tile
    exact = tile.astype(F32)
    quarter = lax.div(lax.broadcasted_iota(jnp.int32, (HALO, TILE), 1), HALO)

    def by_quarter(parts):
        return jnp.where(
            quarter < 2,
            jnp.where(quarter == 0, parts[0], parts[1]),
            jnp.where(quarter == 2, parts[2], parts[3]),
        )

    def turn(x, quarters):
        return pltpu.roll(x, quarters % 4 * HALO, 1) if quarters % 4 else x

    bands = [exact[q * HALO : (q + 1) * HALO] for q in range(4)]
    heads[...] = by_quarter([turn(bands[q], q) for q in range(4)]).astype(BF16)
    tails[...] = by_quarter([turn(bands[q], q - 3) for q in range(4)]).astype(BF16)

    first, last = slice(0, HALO), slice(TILE - HALO, TILE)
    parts = (
        (tile_ref.at[first], south),
        (tile_ref.at[last], north),
        (heads, east.at[1]),
        (tails, west.at[1]),
        (heads, east.at[2]),
        (tails, west.at[2]),
        (heads, east.at[0]),
        (tails, west.at[0]),
    )
    opposite = (1, 0, 3, 2, 7, 6, 5, 4)

    def halo(d):
        row, col = neighbour(d)
        return pltpu.make_async_remote_copy(
            src_ref=parts[d][0],
            dst_ref=parts[d][1],
            send_sem=halo_send.at[d],
            recv_sem=halo_recv.at[d],
            device_id={"row": row, "col": col},
            device_id_type=MESH,
        )

    for d in (2, 3, 4, 5, 6, 7, 0, 1):

        @pl.when(present(d))
        def _(d=d):
            halo(d).start()

    loads[2].wait()
    build_toeplitz(profile_ref, table, inner, outer)

    def empty(lines):
        return jnp.zeros((lines, TILE), F32)

    def sweep(products):
        def step(i, sums):
            product = products(pl.ds(pl.multiple_of((3 - i) * 2 * TILE, 2 * TILE), 2 * TILE))
            tall = product.shape[0]
            odd = pltpu.roll(product[:, TILE:], tall - 1, 0)
            return pltpu.roll(sums, tall - 2, 0) + product[:, :TILE] + odd

        return lax.fori_loop(0, 4, step, jnp.zeros((TILE + 16, TILE), F32), unroll=True)[:TILE]

    def dot(a, b):
        return jnp.dot(a, b, preferred_element_type=F32)

    shifted[:, :TILE] = jnp.concatenate([empty(HALO), exact, empty(HALO)], axis=0).astype(BF16)
    shifted[:, TILE:] = jnp.concatenate(
        [empty(HALO - 8), exact, empty(HALO + 8)], axis=0
    ).astype(BF16)
    own[...] = sweep(
        lambda columns: sum(
            dot(shifted[16 * v : 16 * v + TILE + 16, :], inner[v, :, columns]) for v in range(4)
        )
    )

    for d in range(8):

        @pl.when(present(opposite[d]))
        def _(d=d):
            halo(d).wait_recv()

    tall = TILE + 2 * HALO
    lanes = lax.broadcasted_iota(jnp.int32, (tall, TILE), 1)
    wests = [west[i].astype(F32) for i in range(3)]
    easts = [east[i].astype(F32) for i in range(3)]

    def band(i, q):
        return by_quarter(
            [turn(wests[i], -q), turn(easts[i], 1 - q), turn(wests[i], 2 - q), turn(easts[i], 3 - q)]
        )

    side = jnp.concatenate([band(0, 3)] + [band(1, q) for q in range(4)] + [band(2, 0)], axis=0)
    side_later = jnp.concatenate([side[8:], empty(8)], axis=0)
    sides = jnp.where(lanes < 2 * HALO, side, side_later).astype(BF16)
    beside[:, :TILE] = sides[: tall - 16]
    beside[:, TILE:] = sides[16:]
    above = north[...].astype(F32)
    below = south[...].astype(F32)
    before = jnp.concatenate(
        [above, jnp.concatenate([above[8:], empty(8)], axis=0)], axis=1
    ).astype(BF16)
    after = jnp.concatenate(
        [jnp.concatenate([empty(8), below[:-8]], axis=0), below], axis=1
    ).astype(BF16)

    def around(columns):
        wide = sum(
            dot(beside[32 * v : 32 * v + TILE + 16, :], outer[v, :, columns]) for v in range(2)
        )
        upper = dot(before, inner[0, :, columns])
        upper_next = dot(before[16:], inner[1, :, columns])
        lower = dot(after, inner[3, :, columns])
        lower_next = dot(after[:16], inner[2, :, columns])
        end = TILE + 8 - HALO
        return jnp.concatenate(
            [
                wide[:16] + upper[:16] + upper_next,
                wide[16:HALO] + upper[16:],
                wide[HALO:end],
                wide[end : end + 16] + lower[:16],
                wide[end + 16 : end + 32] + lower[16:] + lower_next,
                wide[end + 32 :],
            ],
            axis=0,
        )

    edge = table[DISC - 1 : DISC, TILE - HALO : TILE - HALO + 1]
    result = own[...] + jnp.concatenate([exact[HALO:], below], axis=0) * edge + sweep(around)
    out_ref[...] = result * (1.0 / density)

    def drain(target, unused):
        @pl.when(target != mine)
        def _():
            message(mine, device(target)).wait_send()

        return unused

    lax.fori_loop(0, tiles, drain, 0)
    for d in range(8):

        @pl.when(present(d))
        def _(d=d):
            halo(d).wait_send()


def shards(positions, destination, profile):
    rows = lax.axis_size("row")
    cols = lax.axis_size("col")
    tiles = rows * cols
    blocks, _, rays = positions.shape
    density = blocks * rays / (TILE * TILE)
    tall = TILE + 2 * HALO
    vmem = pl.BlockSpec(memory_space=pltpu.VMEM)
    return pl.pallas_call(
        functools.partial(body, rows, cols, density),
        out_shape=pltpu.VMEM((TILE, TILE), F32),
        in_specs=[pl.BlockSpec(memory_space=pltpu.HBM)] * 3,
        out_specs=vmem,
        scratch_shapes=[
            pltpu.VMEM((blocks, 2, rays), F32),
            pltpu.VMEM((1, blocks), jnp.int32),
            pltpu.VMEM((DISC, DISC), F32),
            pltpu.VMEM((tiles, GROUP, 2 * rays // 3), jnp.int32),
            pltpu.VMEM((tiles, GROUP, 2 * rays // 3), jnp.int32),
            pltpu.VMEM((72, TILE), F32),
            pltpu.VMEM((4, 2 * TILE, 8 * TILE), BF16),
            pltpu.VMEM((2, 2 * TILE, 8 * TILE), BF16),
            pltpu.VMEM((TILE, TILE), BF16),
            pltpu.VMEM((HALO, TILE), BF16),
            pltpu.VMEM((HALO, TILE), BF16),
            pltpu.VMEM((3, HALO, TILE), BF16),
            pltpu.VMEM((3, HALO, TILE), BF16),
            pltpu.VMEM((HALO, TILE), BF16),
            pltpu.VMEM((HALO, TILE), BF16),
            pltpu.VMEM((tall, 2 * TILE), BF16),
            pltpu.VMEM((tall - 16, 2 * TILE), BF16),
            pltpu.VMEM((TILE, TILE), F32),
            pltpu.VMEM((TILE, TILE), F32),
            pltpu.SemaphoreType.DMA((tiles,)),
            pltpu.SemaphoreType.DMA((tiles,)),
            pltpu.SemaphoreType.REGULAR((cols,)),
            pltpu.SemaphoreType.DMA((8,)),
            pltpu.SemaphoreType.DMA((8,)),
            pltpu.SemaphoreType.DMA((3,)),
        ],
        compiler_params=pltpu.CompilerParams(
            collective_id=0, has_side_effects=True
        ),
        name="lens_map",
    )(positions, destination.reshape(1, blocks), profile)


def solution(mesh):
    placed = (P(("maps", "row", "col"), None, None), P(("maps", "row", "col"), None), P())
    return jax.shard_map(
        shards, mesh=mesh, in_specs=placed, out_specs=P(("maps", "row"), "col"), check_vma=False
    )
```

```python
import functools

import jax
import jax.numpy as jnp
from jax import lax
from jax.experimental import pallas as pl
from jax.experimental.pallas import tpu as pltpu
from jax.sharding import PartitionSpec as P

TILE = 128
HALO = 32
MOST = 4
DISC = 2 * HALO + 1
GROUP = 2 * MOST
TOGETHER = 8
FRACTION = 14
BITS = 21
BF16 = jnp.bfloat16
F32 = jnp.float32
MESH = pl.DeviceIdType.MESH
SIDES = ((-1, 0), (1, 0), (0, -1), (0, 1), (-1, -1), (-1, 1), (1, -1), (1, 1))


def code(coords):
    scaled = coords * float(1 << FRACTION)
    whole = jnp.floor(scaled)
    fixed = whole.astype(jnp.int32)
    return jnp.where(scaled > whole, fixed | 1, fixed) + 1


def sevens(x):
    return [((x >> shift) & 127).astype(F32).astype(BF16) for shift in (0, 7, 14)]


def choose(destination_ref, tiles):
    blocks = destination_ref.shape[1]
    wide = 6 * blocks
    targets = jnp.concatenate([destination_ref[...]] * 6, axis=1)
    lane = lax.broadcasted_iota(jnp.int32, (1, wide), 1)
    piece = sum((lane >= i * blocks).astype(jnp.int32) for i in range(1, 6))
    onehot = jnp.where(lax.broadcasted_iota(jnp.int32, (tiles, wide), 0) == targets, 1.0, 0.0)
    earlier = jnp.where(
        lax.broadcasted_iota(jnp.int32, (blocks, wide), 0) < lane - piece * blocks, 1.0, 0.0
    )
    before = jnp.dot(
        onehot[:, :blocks].astype(BF16), earlier.astype(BF16), preferred_element_type=F32
    )
    rank = jnp.sum(before * onehot, axis=0, keepdims=True).astype(jnp.int32)
    second = piece >= 3
    slot = targets * GROUP + rank + jnp.where(second, MOST, 0)
    order = jnp.where(second, piece - 3, piece)
    weight = jnp.where(order == 0, 1.0, jnp.where(order == 1, 128.0, 16384.0))
    rows = lax.broadcasted_iota(jnp.int32, (tiles * GROUP, wide), 0)
    return jnp.where(rows == slot, weight, 0.0).astype(BF16)


def pack(positions_ref, chosen, outgoing):
    tiles = outgoing.shape[0]
    third = outgoing.shape[2] // 2
    pieces = [piece for c in range(2) for piece in sevens(code(positions_ref[:, c, :]))]
    picked = jnp.dot(chosen, jnp.concatenate(pieces, axis=0), preferred_element_type=F32)
    picked = picked.astype(jnp.int32).reshape(tiles, GROUP, 3 * third)
    low, high, cut = (picked[:, :, i * third : (i + 1) * third] for i in range(3))
    outgoing[:, :, :third] = low | (cut << BITS)
    outgoing[:, :, third:] = high | ((cut >> (32 - BITS)) << BITS)


def unpack(words):
    third = words.shape[1] // 2
    one, two = words[:, :third], words[:, third:]
    mask = (1 << BITS) - 1
    cut = lax.shift_right_logical(one, BITS) | (lax.shift_right_logical(two, BITS) << (32 - BITS))
    return jnp.concatenate([one & mask, two & mask, cut], axis=1)


def build_toeplitz(profile_ref, table, inner, outer):
    table[...] = jnp.zeros_like(table)
    weights = profile_ref[...]
    down = lax.broadcasted_iota(jnp.int32, weights.shape, 0) - HALO
    across = lax.broadcasted_iota(jnp.int32, weights.shape, 1) - HALO
    weights = jnp.where(down * down + across * across <= HALO * HALO, weights, 0.0)
    total = jnp.sum(jnp.sum(weights, axis=1, keepdims=True), axis=0, keepdims=True)
    table[0:DISC, 0:DISC] = weights / total
    square = (TILE, TILE)
    row = lax.broadcasted_iota(jnp.int32, square, 0)
    column = lax.broadcasted_iota(jnp.int32, square, 1)
    flip = jnp.where((row + column) % TILE == 0, 1.0, 0.0).astype(BF16)
    table[...] = jnp.dot(table[...].astype(BF16), flip, preferred_element_type=F32)
    core_mask = jnp.abs(row - column) <= HALO
    side_row = row[: 2 * HALO]
    side_mask = jnp.where(side_row < HALO, column[: 2 * HALO], TILE - 1 - column[: 2 * HALO]) < 2 * HALO

    def eight(u, unused):
        v, h = lax.div(u, 2), lax.rem(u, 2)
        lines = table[pl.ds(pl.multiple_of(u * 8, 8), 8), :]
        core = pl.ds(pl.multiple_of(h * TILE, TILE), TILE)
        side = pl.ds(pl.multiple_of(lax.rem(u, 4) * 2 * HALO, 2 * HALO), 2 * HALO)
        for s in range(8):
            line = jnp.broadcast_to(lines[s : s + 1, :], square)
            circulant = pltpu.roll(line, 0, 1, stride=1, stride_axis=0)
            turned = jnp.concatenate([circulant[HALO:], circulant[:HALO]], axis=0)
            columns = slice(s * TILE, (s + 1) * TILE)
            inner[v, core, columns] = jnp.where(core_mask, turned, 0.0).astype(BF16)
            outer[lax.div(u, 4), side, columns] = jnp.where(side_mask, circulant[: 2 * HALO], 0.0).astype(BF16)
        return unused

    lax.fori_loop(0, 8, eight, 0)


def deposit_group(group, cells, total):
    fixed = unpack(group)
    filled = fixed > 0
    fixed = fixed - 1
    part = (fixed & ((1 << FRACTION) - 1)).astype(F32) * (1.0 / (1 << FRACTION))
    low = (fixed >> FRACTION).astype(F32).astype(BF16)
    here = (1.0 - part).astype(BF16)
    there = jnp.where(filled, part, 0.0).astype(BF16)
    rays = fixed.shape[1]
    packed = (1, 16, rays)
    zero = jnp.zeros((), BF16)
    earlier = cells - jnp.ones((), BF16)

    def row(x, k):
        return jnp.broadcast_to(x[k : k + 1, :], packed[1:]).reshape(packed)

    def hat(k):
        base, upper, lower = row(low, k), row(here, k), row(there, k)
        pieces = jnp.where(cells == base, upper, jnp.where(earlier == base, lower, zero))
        return pieces.reshape(TILE, rays)

    first = jnp.concatenate([hat(m) for m in range(MOST)], axis=1)
    second = jnp.concatenate([hat(MOST + m) for m in range(MOST)], axis=1)
    return total + lax.dot_general(
        first, second, (((1,), (1,)), ((), ())), preferred_element_type=F32
    )


def body(
    rows,
    cols,
    density,
    positions_hbm,
    destination_hbm,
    profile_hbm,
    out_ref,
    positions_ref,
    destination_ref,
    profile_ref,
    outgoing,
    received,
    table,
    inner,
    outer,
    tile_ref,
    north,
    south,
    west,
    east,
    heads,
    tails,
    shifted,
    beside,
    own,
    total,
    send_sems,
    recv_sems,
    notices,
    halo_send,
    halo_recv,
    load_sems,
):
    tiles = rows * cols
    my_row = lax.axis_index("row")
    my_col = lax.axis_index("col")
    me = my_row * cols + my_col
    mine = my_col * rows + my_row

    loads = [
        pltpu.make_async_copy(source, target, load_sems.at[i])
        for i, (source, target) in enumerate(
            (
                (destination_hbm, destination_ref),
                (positions_hbm, positions_ref),
                (profile_hbm, profile_ref),
            )
        )
    ]
    for load in loads:
        load.start()

    def message(source, at):
        target = at["col"] * rows + at["row"]
        return pltpu.make_async_remote_copy(
            src_ref=outgoing.at[at["row"] * cols + at["col"]],
            dst_ref=received.at[source],
            send_sem=send_sems.at[target],
            recv_sem=recv_sems.at[source],
            device_id=at,
            device_id_type=MESH,
        )

    here = {"row": my_row, "col": my_col}

    def device(order):
        return {"row": lax.rem(order, rows), "col": lax.div(order, rows)}

    barrier = pltpu.get_barrier_semaphore()

    def greet(target, unused):
        pl.semaphore_signal(barrier, inc=1, device_id=device(target), device_id_type=MESH)
        return unused

    lax.fori_loop(mine + 1, tiles, greet, 0)

    def settle(semaphore, count):
        @pl.when(count > 0)
        def _():
            pl.semaphore_wait(semaphore, count)

    settle(barrier, mine)

    def tell(at):
        pl.semaphore_signal(notices.at[my_col], inc=1, device_id=at, device_id_type=MESH)

    def lower(act):
        def column(col, unused):
            for row in reversed(range(rows)):
                act({"row": row, "col": col})
            return unused

        def inside(row, unused):
            act({"row": row, "col": my_col})
            return unused

        lax.fori_loop(0, my_col, column, 0)
        lax.fori_loop(0, my_row, inside, 0)

    lower(tell)
    loads[0].wait()
    chosen = choose(destination_ref, tiles)
    loads[1].wait()
    pack(positions_ref, chosen, outgoing)

    def start(at):
        message(mine, at).start()

    lower(start)

    def send_up(col, unused):
        first = jnp.where(col == my_col, my_row + 1, 0)
        settle(notices.at[col], rows - first)

        def each(row, done):
            start({"row": row, "col": col})
            return done

        lax.fori_loop(first, rows, each, 0)

        return unused

    lax.fori_loop(my_col, cols, send_up, 0)
    near = rows * (2 if cols % 2 == 0 else 1)
    base = lax.div(mine, near) * near
    ceiling = base + near

    def partner(j):
        ahead = mine + j
        within = jnp.where(ahead >= ceiling, ahead - near, ahead)
        rest = j - near
        return jnp.where(j < near, within, jnp.where(rest < base, base - 1 - rest, j))

    def neighbour(d):
        down, right = SIDES[d]
        return my_row + down, my_col + right

    def present(d):
        row, col = neighbour(d)
        return (row >= 0) & (row < rows) & (col >= 0) & (col < cols)

    places = (
        north,
        south,
        west.at[1],
        east.at[1],
        west.at[0],
        east.at[0],
        west.at[2],
        east.at[2],
    )
    for d in range(8):

        @pl.when(jnp.logical_not(present(d)))
        def _(d=d):
            places[d][...] = jnp.zeros(places[d].shape, BF16)

    rays = positions_ref.shape[2]
    cell_shape = (TILE // 16, 16, rays)
    cells = (
        lax.broadcasted_iota(jnp.int32, cell_shape, 0) * 16
        + lax.broadcasted_iota(jnp.int32, cell_shape, 1)
    ).astype(F32)
    cells = cells.astype(BF16)
    received[mine] = outgoing[me]
    total[...] = jnp.zeros((TILE, TILE), F32)

    def take(i, unused):
        sources = [partner(TOGETHER * i + j) for j in range(TOGETHER)]
        for source in sources:

            @pl.when(source != mine)
            def _(source=source):
                message(source, here).wait_recv()

        partial = total[...]
        for source in sources:
            partial = deposit_group(received[source], cells, partial)
        total[...] = partial
        return unused

    lax.fori_loop(0, tiles // TOGETHER, take, 0)

    tile = total[...].astype(BF16)
    tile_ref[...] = tile
    exact = tile.astype(F32)
    quarter = lax.div(lax.broadcasted_iota(jnp.int32, (HALO, TILE), 1), HALO)

    def by_quarter(parts):
        return jnp.where(
            quarter < 2,
            jnp.where(quarter == 0, parts[0], parts[1]),
            jnp.where(quarter == 2, parts[2], parts[3]),
        )

    def turn(x, quarters):
        return pltpu.roll(x, quarters % 4 * HALO, 1) if quarters % 4 else x

    bands = [exact[q * HALO : (q + 1) * HALO] for q in range(4)]
    heads[...] = by_quarter([turn(bands[q], q) for q in range(4)]).astype(BF16)
    tails[...] = by_quarter([turn(bands[q], q - 3) for q in range(4)]).astype(BF16)

    first, last = slice(0, HALO), slice(TILE - HALO, TILE)
    parts = (
        (tile_ref.at[first], south),
        (tile_ref.at[last], north),
        (heads, east.at[1]),
        (tails, west.at[1]),
        (heads, east.at[2]),
        (tails, west.at[2]),
        (heads, east.at[0]),
        (tails, west.at[0]),
    )
    opposite = (1, 0, 3, 2, 7, 6, 5, 4)

    def halo(d):
        row, col = neighbour(d)
        return pltpu.make_async_remote_copy(
            src_ref=parts[d][0],
            dst_ref=parts[d][1],
            send_sem=halo_send.at[d],
            recv_sem=halo_recv.at[d],
            device_id={"row": row, "col": col},
            device_id_type=MESH,
        )

    for d in (2, 3, 4, 5, 6, 7, 0, 1):

        @pl.when(present(d))
        def _(d=d):
            halo(d).start()

    loads[2].wait()
    build_toeplitz(profile_ref, table, inner, outer)

    def empty(lines):
        return jnp.zeros((lines, TILE), F32)

    def sweep(products):
        def step(i, sums):
            product = products(pl.ds(pl.multiple_of((3 - i) * 2 * TILE, 2 * TILE), 2 * TILE))
            tall = product.shape[0]
            odd = pltpu.roll(product[:, TILE:], tall - 1, 0)
            return pltpu.roll(sums, tall - 2, 0) + product[:, :TILE] + odd

        return lax.fori_loop(0, 4, step, jnp.zeros((TILE + 16, TILE), F32), unroll=True)[:TILE]

    def dot(a, b):
        return jnp.dot(a, b, preferred_element_type=F32)

    shifted[:, :TILE] = jnp.concatenate([empty(HALO), exact, empty(HALO)], axis=0).astype(BF16)
    shifted[:, TILE:] = jnp.concatenate(
        [empty(HALO - 8), exact, empty(HALO + 8)], axis=0
    ).astype(BF16)
    own[...] = sweep(
        lambda columns: sum(
            dot(shifted[16 * v : 16 * v + TILE + 16, :], inner[v, :, columns]) for v in range(4)
        )
    )

    def drain(target, unused):
        @pl.when(target != mine)
        def _():
            message(mine, device(target)).wait_send()

        return unused

    lax.fori_loop(0, tiles, drain, 0)

    for d in range(8):

        @pl.when(present(opposite[d]))
        def _(d=d):
            halo(d).wait_recv()

    tall = TILE + 2 * HALO
    lanes = lax.broadcasted_iota(jnp.int32, (tall, TILE), 1)
    wests = [west[i].astype(F32) for i in range(3)]
    easts = [east[i].astype(F32) for i in range(3)]

    def band(i, q):
        return by_quarter(
            [turn(wests[i], -q), turn(easts[i], 1 - q), turn(wests[i], 2 - q), turn(easts[i], 3 - q)]
        )

    side = jnp.concatenate([band(0, 3)] + [band(1, q) for q in range(4)] + [band(2, 0)], axis=0)
    side_later = jnp.concatenate([side[8:], empty(8)], axis=0)
    sides = jnp.where(lanes < 2 * HALO, side, side_later).astype(BF16)
    beside[:, :TILE] = sides[: tall - 16]
    beside[:, TILE:] = sides[16:]
    above = north[...].astype(F32)
    below = south[...].astype(F32)
    before = jnp.concatenate(
        [above, jnp.concatenate([above[8:], empty(8)], axis=0)], axis=1
    ).astype(BF16)
    after = jnp.concatenate(
        [jnp.concatenate([empty(8), below[:-8]], axis=0), below], axis=1
    ).astype(BF16)

    def around(columns):
        wide = sum(
            dot(beside[32 * v : 32 * v + TILE + 16, :], outer[v, :, columns]) for v in range(2)
        )
        upper = dot(before, inner[0, :, columns])
        upper_next = dot(before[16:], inner[1, :, columns])
        lower = dot(after, inner[3, :, columns])
        lower_next = dot(after[:16], inner[2, :, columns])
        end = TILE + 8 - HALO
        return jnp.concatenate(
            [
                wide[:16] + upper[:16] + upper_next,
                wide[16:HALO] + upper[16:],
                wide[HALO:end],
                wide[end : end + 16] + lower[:16],
                wide[end + 16 : end + 32] + lower[16:] + lower_next,
                wide[end + 32 :],
            ],
            axis=0,
        )

    edge = table[DISC - 1 : DISC, TILE - HALO : TILE - HALO + 1]
    result = own[...] + jnp.concatenate([exact[HALO:], below], axis=0) * edge + sweep(around)
    out_ref[...] = result * (1.0 / density)

    for d in range(8):

        @pl.when(present(d))
        def _(d=d):
            halo(d).wait_send()


def shards(positions, destination, profile):
    rows = lax.axis_size("row")
    cols = lax.axis_size("col")
    tiles = rows * cols
    blocks, _, rays = positions.shape
    density = blocks * rays / (TILE * TILE)
    tall = TILE + 2 * HALO
    vmem = pl.BlockSpec(memory_space=pltpu.VMEM)
    return pl.pallas_call(
        functools.partial(body, rows, cols, density),
        out_shape=pltpu.VMEM((TILE, TILE), F32),
        in_specs=[pl.BlockSpec(memory_space=pltpu.HBM)] * 3,
        out_specs=vmem,
        scratch_shapes=[
            pltpu.VMEM((blocks, 2, rays), F32),
            pltpu.VMEM((1, blocks), jnp.int32),
            pltpu.VMEM((DISC, DISC), F32),
            pltpu.VMEM((tiles, GROUP, 2 * rays // 3), jnp.int32),
            pltpu.VMEM((tiles, GROUP, 2 * rays // 3), jnp.int32),
            pltpu.VMEM((72, TILE), F32),
            pltpu.VMEM((4, 2 * TILE, 8 * TILE), BF16),
            pltpu.VMEM((2, 2 * TILE, 8 * TILE), BF16),
            pltpu.VMEM((TILE, TILE), BF16),
            pltpu.VMEM((HALO, TILE), BF16),
            pltpu.VMEM((HALO, TILE), BF16),
            pltpu.VMEM((3, HALO, TILE), BF16),
            pltpu.VMEM((3, HALO, TILE), BF16),
            pltpu.VMEM((HALO, TILE), BF16),
            pltpu.VMEM((HALO, TILE), BF16),
            pltpu.VMEM((tall, 2 * TILE), BF16),
            pltpu.VMEM((tall - 16, 2 * TILE), BF16),
            pltpu.VMEM((TILE, TILE), F32),
            pltpu.VMEM((TILE, TILE), F32),
            pltpu.SemaphoreType.DMA((tiles,)),
            pltpu.SemaphoreType.DMA((tiles,)),
            pltpu.SemaphoreType.REGULAR((cols,)),
            pltpu.SemaphoreType.DMA((8,)),
            pltpu.SemaphoreType.DMA((8,)),
            pltpu.SemaphoreType.DMA((3,)),
        ],
        compiler_params=pltpu.CompilerParams(
            collective_id=0, has_side_effects=True
        ),
        name="lens_map",
    )(positions, destination.reshape(1, blocks), profile)


def solution(mesh):
    placed = (P(("maps", "row", "col"), None, None), P(("maps", "row", "col"), None), P())
    return jax.shard_map(
        shards, mesh=mesh, in_specs=placed, out_specs=P(("maps", "row"), "col"), check_vma=False
    )
```

```python
import functools

import jax
import jax.numpy as jnp
from jax import lax
from jax.experimental import pallas as pl
from jax.experimental.pallas import tpu as pltpu
from jax.sharding import PartitionSpec as P

TILE = 128
HALO = 32
MOST = 4
DISC = 2 * HALO + 1
GROUP = 2 * MOST
TOGETHER = 8
FRACTION = 14
BITS = 21
BF16 = jnp.bfloat16
F32 = jnp.float32
MESH = pl.DeviceIdType.MESH
SIDES = ((-1, 0), (1, 0), (0, -1), (0, 1), (-1, -1), (-1, 1), (1, -1), (1, 1))


def code(coords):
    scaled = coords * float(1 << FRACTION)
    whole = jnp.floor(scaled)
    fixed = whole.astype(jnp.int32)
    return jnp.where(scaled > whole, fixed | 1, fixed) + 1


def sevens(x):
    return [((x >> shift) & 127).astype(F32).astype(BF16) for shift in (0, 7, 14)]


def choose(destination_ref, tiles):
    blocks = destination_ref.shape[1]
    wide = 6 * blocks
    targets = jnp.concatenate([destination_ref[...]] * 6, axis=1)
    lane = lax.broadcasted_iota(jnp.int32, (1, wide), 1)
    piece = sum((lane >= i * blocks).astype(jnp.int32) for i in range(1, 6))
    onehot = jnp.where(lax.broadcasted_iota(jnp.int32, (tiles, wide), 0) == targets, 1.0, 0.0)
    earlier = jnp.where(
        lax.broadcasted_iota(jnp.int32, (blocks, wide), 0) < lane - piece * blocks, 1.0, 0.0
    )
    before = jnp.dot(
        onehot[:, :blocks].astype(BF16), earlier.astype(BF16), preferred_element_type=F32
    )
    rank = jnp.sum(before * onehot, axis=0, keepdims=True).astype(jnp.int32)
    second = piece >= 3
    slot = targets * GROUP + rank + jnp.where(second, MOST, 0)
    order = jnp.where(second, piece - 3, piece)
    weight = jnp.where(order == 0, 1.0, jnp.where(order == 1, 128.0, 16384.0))
    rows = lax.broadcasted_iota(jnp.int32, (tiles * GROUP, wide), 0)
    return jnp.where(rows == slot, weight, 0.0).astype(BF16)


def pack(positions_ref, chosen, outgoing):
    tiles = outgoing.shape[0]
    third = outgoing.shape[2] // 2
    pieces = [piece for c in range(2) for piece in sevens(code(positions_ref[:, c, :]))]
    picked = jnp.dot(chosen, jnp.concatenate(pieces, axis=0), preferred_element_type=F32)
    picked = picked.astype(jnp.int32).reshape(tiles, GROUP, 3 * third)
    low, high, cut = (picked[:, :, i * third : (i + 1) * third] for i in range(3))
    outgoing[:, :, :third] = low | (cut << BITS)
    outgoing[:, :, third:] = high | ((cut >> (32 - BITS)) << BITS)


def unpack(words):
    third = words.shape[1] // 2
    one, two = words[:, :third], words[:, third:]
    mask = (1 << BITS) - 1
    cut = lax.shift_right_logical(one, BITS) | (lax.shift_right_logical(two, BITS) << (32 - BITS))
    return jnp.concatenate([one & mask, two & mask, cut], axis=1)


def build_toeplitz(profile_ref, table, inner, outer):
    table[...] = jnp.zeros_like(table)
    weights = profile_ref[...]
    down = lax.broadcasted_iota(jnp.int32, weights.shape, 0) - HALO
    across = lax.broadcasted_iota(jnp.int32, weights.shape, 1) - HALO
    weights = jnp.where(down * down + across * across <= HALO * HALO, weights, 0.0)
    total = jnp.sum(jnp.sum(weights, axis=1, keepdims=True), axis=0, keepdims=True)
    table[0:DISC, 0:DISC] = weights / total
    square = (TILE, TILE)
    row = lax.broadcasted_iota(jnp.int32, square, 0)
    column = lax.broadcasted_iota(jnp.int32, square, 1)
    flip = jnp.where((row + column) % TILE == 0, 1.0, 0.0).astype(BF16)
    table[...] = jnp.dot(table[...].astype(BF16), flip, preferred_element_type=F32)
    core_mask = jnp.abs(row - column) <= HALO
    side_row = row[: 2 * HALO]
    side_mask = jnp.where(side_row < HALO, column[: 2 * HALO], TILE - 1 - column[: 2 * HALO]) < 2 * HALO

    def eight(u, unused):
        v, h = lax.div(u, 2), lax.rem(u, 2)
        lines = table[pl.ds(pl.multiple_of(u * 8, 8), 8), :]
        core = pl.ds(pl.multiple_of(h * TILE, TILE), TILE)
        side = pl.ds(pl.multiple_of(lax.rem(u, 4) * 2 * HALO, 2 * HALO), 2 * HALO)
        for s in range(8):
            line = jnp.broadcast_to(lines[s : s + 1, :], square)
            circulant = pltpu.roll(line, 0, 1, stride=1, stride_axis=0)
            turned = jnp.concatenate([circulant[HALO:], circulant[:HALO]], axis=0)
            columns = slice(s * TILE, (s + 1) * TILE)
            inner[v, core, columns] = jnp.where(core_mask, turned, 0.0).astype(BF16)
            outer[lax.div(u, 4), side, columns] = jnp.where(side_mask, circulant[: 2 * HALO], 0.0).astype(BF16)
        return unused

    lax.fori_loop(0, 8, eight, 0)


def deposit_group(group, cells, total):
    fixed = unpack(group)
    filled = fixed > 0
    fixed = fixed - 1
    part = (fixed & ((1 << FRACTION) - 1)).astype(F32) * (1.0 / (1 << FRACTION))
    low = (fixed >> FRACTION).astype(F32).astype(BF16)
    here = (1.0 - part).astype(BF16)
    there = jnp.where(filled, part, 0.0).astype(BF16)
    rays = fixed.shape[1]
    packed = (1, 16, rays)
    zero = jnp.zeros((), BF16)
    earlier = cells - jnp.ones((), BF16)

    def row(x, k):
        return jnp.broadcast_to(x[k : k + 1, :], packed[1:]).reshape(packed)

    def hat(k):
        base, upper, lower = row(low, k), row(here, k), row(there, k)
        pieces = jnp.where(cells == base, upper, jnp.where(earlier == base, lower, zero))
        return pieces.reshape(TILE, rays)

    first = jnp.concatenate([hat(m) for m in range(MOST)], axis=1)
    second = jnp.concatenate([hat(MOST + m) for m in range(MOST)], axis=1)
    return total + lax.dot_general(
        first, second, (((1,), (1,)), ((), ())), preferred_element_type=F32
    )


def body(
    rows,
    cols,
    density,
    positions_hbm,
    destination_hbm,
    profile_hbm,
    out_ref,
    positions_ref,
    destination_ref,
    profile_ref,
    outgoing,
    received,
    table,
    inner,
    outer,
    tile_ref,
    north,
    south,
    west,
    east,
    heads,
    tails,
    shifted,
    beside,
    own,
    total,
    send_sems,
    recv_sems,
    notices,
    halo_send,
    halo_recv,
    load_sems,
):
    tiles = rows * cols
    my_row = lax.axis_index("row")
    my_col = lax.axis_index("col")
    me = my_row * cols + my_col
    mine = my_col * rows + my_row

    loads = [
        pltpu.make_async_copy(source, target, load_sems.at[i])
        for i, (source, target) in enumerate(
            (
                (destination_hbm, destination_ref),
                (positions_hbm, positions_ref),
                (profile_hbm, profile_ref),
            )
        )
    ]
    for load in loads:
        load.start()

    def message(source, at):
        target = at["col"] * rows + at["row"]
        return pltpu.make_async_remote_copy(
            src_ref=outgoing.at[at["row"] * cols + at["col"]],
            dst_ref=received.at[source],
            send_sem=send_sems.at[target],
            recv_sem=recv_sems.at[source],
            device_id=at,
            device_id_type=MESH,
        )

    here = {"row": my_row, "col": my_col}

    def device(order):
        return {"row": lax.rem(order, rows), "col": lax.div(order, rows)}

    barrier = pltpu.get_barrier_semaphore()

    def greet(target, unused):
        pl.semaphore_signal(barrier, inc=1, device_id=device(target), device_id_type=MESH)
        return unused

    lax.fori_loop(mine + 1, tiles, greet, 0)

    def settle(semaphore, count):
        @pl.when(count > 0)
        def _():
            pl.semaphore_wait(semaphore, count)

    settle(barrier, mine)

    def tell(at):
        pl.semaphore_signal(notices.at[my_col], inc=1, device_id=at, device_id_type=MESH)

    def lower(act):
        def column(col, unused):
            for row in reversed(range(rows)):
                act({"row": row, "col": col})
            return unused

        def inside(row, unused):
            act({"row": row, "col": my_col})
            return unused

        lax.fori_loop(0, my_col, column, 0)
        lax.fori_loop(0, my_row, inside, 0)

    lower(tell)
    loads[0].wait()
    chosen = choose(destination_ref, tiles)
    loads[1].wait()
    pack(positions_ref, chosen, outgoing)

    def start(at):
        message(mine, at).start()

    lower(start)

    def send_up(col, unused):
        first = jnp.where(col == my_col, my_row + 1, 0)
        settle(notices.at[col], rows - first)

        def each(row, done):
            start({"row": row, "col": col})
            return done

        lax.fori_loop(first, rows, each, 0)

        return unused

    lax.fori_loop(my_col, cols, send_up, 0)
    near = rows * (2 if cols % 2 == 0 else 1)
    base = lax.div(mine, near) * near
    ceiling = base + near

    def partner(j):
        ahead = mine + j
        within = jnp.where(ahead >= ceiling, ahead - near, ahead)
        rest = j - near
        return jnp.where(j < near, within, jnp.where(rest < base, base - 1 - rest, j))

    def neighbour(d):
        down, right = SIDES[d]
        return my_row + down, my_col + right

    def present(d):
        row, col = neighbour(d)
        return (row >= 0) & (row < rows) & (col >= 0) & (col < cols)

    places = (
        north,
        south,
        west.at[1],
        east.at[1],
        west.at[0],
        east.at[0],
        west.at[2],
        east.at[2],
    )
    for d in range(8):

        @pl.when(jnp.logical_not(present(d)))
        def _(d=d):
            places[d][...] = jnp.zeros(places[d].shape, BF16)

    rays = positions_ref.shape[2]
    cell_shape = (TILE // 16, 16, rays)
    cells = (
        lax.broadcasted_iota(jnp.int32, cell_shape, 0) * 16
        + lax.broadcasted_iota(jnp.int32, cell_shape, 1)
    ).astype(F32)
    cells = cells.astype(BF16)
    received[mine] = outgoing[me]
    total[...] = jnp.zeros((TILE, TILE), F32)

    def take(i, unused):
        sources = [partner(TOGETHER * i + j) for j in range(TOGETHER)]
        for source in sources:

            @pl.when(source != mine)
            def _(source=source):
                message(source, here).wait_recv()

        partial = total[...]
        for source in sources:
            partial = deposit_group(received[source], cells, partial)
        total[...] = partial
        return unused

    lax.fori_loop(0, tiles // TOGETHER, take, 0)

    tile = total[...].astype(BF16)
    tile_ref[...] = tile
    exact = tile.astype(F32)
    quarter = lax.div(lax.broadcasted_iota(jnp.int32, (HALO, TILE), 1), HALO)

    def by_quarter(parts):
        return jnp.where(
            quarter < 2,
            jnp.where(quarter == 0, parts[0], parts[1]),
            jnp.where(quarter == 2, parts[2], parts[3]),
        )

    def turn(x, quarters):
        return pltpu.roll(x, quarters % 4 * HALO, 1) if quarters % 4 else x

    bands = [exact[q * HALO : (q + 1) * HALO] for q in range(4)]
    heads[...] = by_quarter([turn(bands[q], q) for q in range(4)]).astype(BF16)
    tails[...] = by_quarter([turn(bands[q], q - 3) for q in range(4)]).astype(BF16)

    first, last = slice(0, HALO), slice(TILE - HALO, TILE)
    parts = (
        (tile_ref.at[first], south),
        (tile_ref.at[last], north),
        (heads, east.at[1]),
        (tails, west.at[1]),
        (heads, east.at[2]),
        (tails, west.at[2]),
        (heads, east.at[0]),
        (tails, west.at[0]),
    )
    opposite = (1, 0, 3, 2, 7, 6, 5, 4)

    def halo(d):
        row, col = neighbour(d)
        return pltpu.make_async_remote_copy(
            src_ref=parts[d][0],
            dst_ref=parts[d][1],
            send_sem=halo_send.at[d],
            recv_sem=halo_recv.at[d],
            device_id={"row": row, "col": col},
            device_id_type=MESH,
        )

    for d in (2, 3, 4, 5, 6, 7, 0, 1):

        @pl.when(present(d))
        def _(d=d):
            halo(d).start()

    loads[2].wait()
    build_toeplitz(profile_ref, table, inner, outer)

    def empty(lines):
        return jnp.zeros((lines, TILE), F32)

    def sweep(products):
        def step(i, sums):
            product = products(pl.ds(pl.multiple_of((3 - i) * 2 * TILE, 2 * TILE), 2 * TILE))
            tall = product.shape[0]
            odd = pltpu.roll(product[:, TILE:], tall - 1, 0)
            return pltpu.roll(sums, tall - 2, 0) + product[:, :TILE] + odd

        return lax.fori_loop(0, 4, step, jnp.zeros((TILE + 16, TILE), F32), unroll=True)[:TILE]

    def dot(a, b):
        return jnp.dot(a, b, preferred_element_type=F32)

    shifted[:, :TILE] = jnp.concatenate([empty(HALO), exact, empty(HALO)], axis=0).astype(BF16)
    shifted[:, TILE:] = jnp.concatenate(
        [empty(HALO - 8), exact, empty(HALO + 8)], axis=0
    ).astype(BF16)
    own[...] = sweep(
        lambda columns: sum(
            dot(shifted[16 * v : 16 * v + TILE + 16, :], inner[v, :, columns]) for v in range(4)
        )
    )

    def drain(target, unused):
        @pl.when(target != mine)
        def _():
            message(mine, device(target)).wait_send()

        return unused

    lax.fori_loop(0, tiles, drain, 0)

    for d in range(8):

        @pl.when(present(d))
        def _(d=d):
            halo(d).wait_send()
            halo(opposite[d]).wait_recv()

    tall = TILE + 2 * HALO
    lanes = lax.broadcasted_iota(jnp.int32, (tall, TILE), 1)
    wests = [west[i].astype(F32) for i in range(3)]
    easts = [east[i].astype(F32) for i in range(3)]

    def band(i, q):
        return by_quarter(
            [turn(wests[i], -q), turn(easts[i], 1 - q), turn(wests[i], 2 - q), turn(easts[i], 3 - q)]
        )

    side = jnp.concatenate([band(0, 3)] + [band(1, q) for q in range(4)] + [band(2, 0)], axis=0)
    side_later = jnp.concatenate([side[8:], empty(8)], axis=0)
    sides = jnp.where(lanes < 2 * HALO, side, side_later).astype(BF16)
    beside[:, :TILE] = sides[: tall - 16]
    beside[:, TILE:] = sides[16:]
    above = north[...].astype(F32)
    below = south[...].astype(F32)
    before = jnp.concatenate(
        [above, jnp.concatenate([above[8:], empty(8)], axis=0)], axis=1
    ).astype(BF16)
    after = jnp.concatenate(
        [jnp.concatenate([empty(8), below[:-8]], axis=0), below], axis=1
    ).astype(BF16)

    def around(columns):
        wide = sum(
            dot(beside[32 * v : 32 * v + TILE + 16, :], outer[v, :, columns]) for v in range(2)
        )
        upper = dot(before, inner[0, :, columns])
        upper_next = dot(before[16:], inner[1, :, columns])
        lower = dot(after, inner[3, :, columns])
        lower_next = dot(after[:16], inner[2, :, columns])
        end = TILE + 8 - HALO
        return jnp.concatenate(
            [
                wide[:16] + upper[:16] + upper_next,
                wide[16:HALO] + upper[16:],
                wide[HALO:end],
                wide[end : end + 16] + lower[:16],
                wide[end + 16 : end + 32] + lower[16:] + lower_next,
                wide[end + 32 :],
            ],
            axis=0,
        )

    edge = table[DISC - 1 : DISC, TILE - HALO : TILE - HALO + 1]
    result = own[...] + jnp.concatenate([exact[HALO:], below], axis=0) * edge + sweep(around)
    out_ref[...] = result * (1.0 / density)


def shards(positions, destination, profile):
    rows = lax.axis_size("row")
    cols = lax.axis_size("col")
    tiles = rows * cols
    blocks, _, rays = positions.shape
    density = blocks * rays / (TILE * TILE)
    tall = TILE + 2 * HALO
    vmem = pl.BlockSpec(memory_space=pltpu.VMEM)
    return pl.pallas_call(
        functools.partial(body, rows, cols, density),
        out_shape=pltpu.VMEM((TILE, TILE), F32),
        in_specs=[pl.BlockSpec(memory_space=pltpu.HBM)] * 3,
        out_specs=vmem,
        scratch_shapes=[
            pltpu.VMEM((blocks, 2, rays), F32),
            pltpu.VMEM((1, blocks), jnp.int32),
            pltpu.VMEM((DISC, DISC), F32),
            pltpu.VMEM((tiles, GROUP, 2 * rays // 3), jnp.int32),
            pltpu.VMEM((tiles, GROUP, 2 * rays // 3), jnp.int32),
            pltpu.VMEM((72, TILE), F32),
            pltpu.VMEM((4, 2 * TILE, 8 * TILE), BF16),
            pltpu.VMEM((2, 2 * TILE, 8 * TILE), BF16),
            pltpu.VMEM((TILE, TILE), BF16),
            pltpu.VMEM((HALO, TILE), BF16),
            pltpu.VMEM((HALO, TILE), BF16),
            pltpu.VMEM((3, HALO, TILE), BF16),
            pltpu.VMEM((3, HALO, TILE), BF16),
            pltpu.VMEM((HALO, TILE), BF16),
            pltpu.VMEM((HALO, TILE), BF16),
            pltpu.VMEM((tall, 2 * TILE), BF16),
            pltpu.VMEM((tall - 16, 2 * TILE), BF16),
            pltpu.VMEM((TILE, TILE), F32),
            pltpu.VMEM((TILE, TILE), F32),
            pltpu.SemaphoreType.DMA((tiles,)),
            pltpu.SemaphoreType.DMA((tiles,)),
            pltpu.SemaphoreType.REGULAR((cols,)),
            pltpu.SemaphoreType.DMA((8,)),
            pltpu.SemaphoreType.DMA((8,)),
            pltpu.SemaphoreType.DMA((3,)),
        ],
        compiler_params=pltpu.CompilerParams(
            collective_id=0, has_side_effects=True
        ),
        name="lens_map",
    )(positions, destination.reshape(1, blocks), profile)


def solution(mesh):
    placed = (P(("maps", "row", "col"), None, None), P(("maps", "row", "col"), None), P())
    return jax.shard_map(
        shards, mesh=mesh, in_specs=placed, out_specs=P(("maps", "row"), "col"), check_vma=False
    )
```

```python
import functools

import jax
import jax.numpy as jnp
from jax import lax
from jax.experimental import pallas as pl
from jax.experimental.pallas import tpu as pltpu
from jax.sharding import PartitionSpec as P

TILE = 128
HALO = 32
MOST = 4
DISC = 2 * HALO + 1
GROUP = 2 * MOST
TOGETHER = 8
FRACTION = 14
BITS = 21
BF16 = jnp.bfloat16
F32 = jnp.float32
MESH = pl.DeviceIdType.MESH
SIDES = ((-1, 0), (1, 0), (0, -1), (0, 1), (-1, -1), (-1, 1), (1, -1), (1, 1))


def code(coords):
    scaled = coords * float(1 << FRACTION)
    whole = jnp.floor(scaled)
    fixed = whole.astype(jnp.int32)
    return jnp.where(scaled > whole, fixed | 1, fixed) + 1


def sevens(x):
    return [((x >> shift) & 127).astype(F32).astype(BF16) for shift in (0, 7, 14)]


def choose(destination_ref, tiles):
    blocks = destination_ref.shape[1]
    wide = 6 * blocks
    targets = jnp.concatenate([destination_ref[...]] * 6, axis=1)
    lane = lax.broadcasted_iota(jnp.int32, (1, wide), 1)
    piece = sum((lane >= i * blocks).astype(jnp.int32) for i in range(1, 6))
    onehot = jnp.where(lax.broadcasted_iota(jnp.int32, (tiles, wide), 0) == targets, 1.0, 0.0)
    earlier = jnp.where(
        lax.broadcasted_iota(jnp.int32, (blocks, wide), 0) < lane - piece * blocks, 1.0, 0.0
    )
    before = jnp.dot(
        onehot[:, :blocks].astype(BF16), earlier.astype(BF16), preferred_element_type=F32
    )
    rank = jnp.sum(before * onehot, axis=0, keepdims=True).astype(jnp.int32)
    second = piece >= 3
    slot = targets * GROUP + rank + jnp.where(second, MOST, 0)
    order = jnp.where(second, piece - 3, piece)
    weight = jnp.where(order == 0, 1.0, jnp.where(order == 1, 128.0, 16384.0))
    rows = lax.broadcasted_iota(jnp.int32, (tiles * GROUP, wide), 0)
    return jnp.where(rows == slot, weight, 0.0).astype(BF16)


def pack(positions_ref, chosen, outgoing):
    tiles = outgoing.shape[0]
    third = outgoing.shape[2] // 2
    pieces = [piece for c in range(2) for piece in sevens(code(positions_ref[:, c, :]))]
    picked = jnp.dot(chosen, jnp.concatenate(pieces, axis=0), preferred_element_type=F32)
    picked = picked.astype(jnp.int32).reshape(tiles, GROUP, 3 * third)
    low, high, cut = (picked[:, :, i * third : (i + 1) * third] for i in range(3))
    outgoing[:, :, :third] = low | (cut << BITS)
    outgoing[:, :, third:] = high | ((cut >> (32 - BITS)) << BITS)


def unpack(words):
    third = words.shape[1] // 2
    one, two = words[:, :third], words[:, third:]
    mask = (1 << BITS) - 1
    cut = lax.shift_right_logical(one, BITS) | (lax.shift_right_logical(two, BITS) << (32 - BITS))
    return jnp.concatenate([one & mask, two & mask, cut], axis=1)


def build_toeplitz(profile_ref, table, inner, outer):
    table[...] = jnp.zeros_like(table)
    weights = profile_ref[...]
    down = lax.broadcasted_iota(jnp.int32, weights.shape, 0) - HALO
    across = lax.broadcasted_iota(jnp.int32, weights.shape, 1) - HALO
    weights = jnp.where(down * down + across * across <= HALO * HALO, weights, 0.0)
    total = jnp.sum(jnp.sum(weights, axis=1, keepdims=True), axis=0, keepdims=True)
    table[0:DISC, 0:DISC] = weights / total
    square = (TILE, TILE)
    row = lax.broadcasted_iota(jnp.int32, square, 0)
    column = lax.broadcasted_iota(jnp.int32, square, 1)
    flip = jnp.where((row + column) % TILE == 0, 1.0, 0.0).astype(BF16)
    table[...] = jnp.dot(table[...].astype(BF16), flip, preferred_element_type=F32)
    core_mask = jnp.abs(row - column) <= HALO
    side_row = row[: 2 * HALO]
    side_mask = jnp.where(side_row < HALO, column[: 2 * HALO], TILE - 1 - column[: 2 * HALO]) < 2 * HALO

    def eight(u, unused):
        v, h = lax.div(u, 2), lax.rem(u, 2)
        lines = table[pl.ds(pl.multiple_of(u * 8, 8), 8), :]
        core = pl.ds(pl.multiple_of(h * TILE, TILE), TILE)
        side = pl.ds(pl.multiple_of(lax.rem(u, 4) * 2 * HALO, 2 * HALO), 2 * HALO)
        for s in range(8):
            line = jnp.broadcast_to(lines[s : s + 1, :], square)
            circulant = pltpu.roll(line, 0, 1, stride=1, stride_axis=0)
            turned = jnp.concatenate([circulant[HALO:], circulant[:HALO]], axis=0)
            columns = slice(s * TILE, (s + 1) * TILE)
            inner[v, core, columns] = jnp.where(core_mask, turned, 0.0).astype(BF16)
            outer[lax.div(u, 4), side, columns] = jnp.where(side_mask, circulant[: 2 * HALO], 0.0).astype(BF16)
        return unused

    lax.fori_loop(0, 8, eight, 0)


def deposit_group(group, cells, total):
    fixed = unpack(group)
    filled = fixed > 0
    fixed = fixed - 1
    part = (fixed & ((1 << FRACTION) - 1)).astype(F32) * (1.0 / (1 << FRACTION))
    low = (fixed >> FRACTION).astype(F32).astype(BF16)
    here = (1.0 - part).astype(BF16)
    there = jnp.where(filled, part, 0.0).astype(BF16)
    rays = fixed.shape[1]
    packed = (1, 16, rays)
    zero = jnp.zeros((), BF16)
    earlier = cells - jnp.ones((), BF16)

    def row(x, k):
        return jnp.broadcast_to(x[k : k + 1, :], packed[1:]).reshape(packed)

    def hat(k):
        base, upper, lower = row(low, k), row(here, k), row(there, k)
        pieces = jnp.where(cells == base, upper, jnp.where(earlier == base, lower, zero))
        return pieces.reshape(TILE, rays)

    first = jnp.concatenate([hat(m) for m in range(MOST)], axis=1)
    second = jnp.concatenate([hat(MOST + m) for m in range(MOST)], axis=1)
    return total + lax.dot_general(
        first, second, (((1,), (1,)), ((), ())), preferred_element_type=F32
    )


def body(
    rows,
    cols,
    density,
    positions_hbm,
    destination_hbm,
    profile_hbm,
    out_ref,
    positions_ref,
    destination_ref,
    profile_ref,
    outgoing,
    received,
    table,
    inner,
    outer,
    tile_ref,
    north,
    south,
    west,
    east,
    heads,
    tails,
    shifted,
    beside,
    own,
    total,
    send_sems,
    recv_sems,
    notices,
    halo_send,
    halo_recv,
    load_sems,
):
    tiles = rows * cols
    my_row = lax.axis_index("row")
    my_col = lax.axis_index("col")
    me = my_row * cols + my_col
    mine = my_col * rows + my_row

    loads = [
        pltpu.make_async_copy(source, target, load_sems.at[i])
        for i, (source, target) in enumerate(
            (
                (destination_hbm, destination_ref),
                (positions_hbm, positions_ref),
                (profile_hbm, profile_ref),
            )
        )
    ]
    for load in loads:
        load.start()

    def message(source, at):
        target = at["col"] * rows + at["row"]
        return pltpu.make_async_remote_copy(
            src_ref=outgoing.at[at["row"] * cols + at["col"]],
            dst_ref=received.at[source],
            send_sem=send_sems.at[target],
            recv_sem=recv_sems.at[source],
            device_id=at,
            device_id_type=MESH,
        )

    here = {"row": my_row, "col": my_col}

    def device(order):
        return {"row": lax.rem(order, rows), "col": lax.div(order, rows)}

    barrier = pltpu.get_barrier_semaphore()

    def greet(target, unused):
        pl.semaphore_signal(barrier, inc=1, device_id=device(target), device_id_type=MESH)
        return unused

    lax.fori_loop(mine + 1, tiles, greet, 0)

    def settle(semaphore, count):
        @pl.when(count > 0)
        def _():
            pl.semaphore_wait(semaphore, count)

    loads[0].wait()
    chosen = choose(destination_ref, tiles)
    settle(barrier, mine)

    def tell(at):
        pl.semaphore_signal(notices.at[my_col], inc=1, device_id=at, device_id_type=MESH)

    def lower(act):
        def column(col, unused):
            for row in reversed(range(rows)):
                act({"row": row, "col": col})
            return unused

        def inside(row, unused):
            act({"row": row, "col": my_col})
            return unused

        lax.fori_loop(0, my_col, column, 0)
        lax.fori_loop(0, my_row, inside, 0)

    lower(tell)
    loads[1].wait()
    pack(positions_ref, chosen, outgoing)

    def start(at):
        message(mine, at).start()

    lower(start)

    def send_up(col, unused):
        first = jnp.where(col == my_col, my_row + 1, 0)
        settle(notices.at[col], rows - first)

        def each(row, done):
            start({"row": row, "col": col})
            return done

        lax.fori_loop(first, rows, each, 0)

        return unused

    lax.fori_loop(my_col, cols, send_up, 0)
    near = rows * (2 if cols % 2 == 0 else 1)
    base = lax.div(mine, near) * near
    ceiling = base + near

    def partner(j):
        ahead = mine + j
        within = jnp.where(ahead >= ceiling, ahead - near, ahead)
        rest = j - near
        return jnp.where(j < near, within, jnp.where(rest < base, base - 1 - rest, j))

    def neighbour(d):
        down, right = SIDES[d]
        return my_row + down, my_col + right

    def present(d):
        row, col = neighbour(d)
        return (row >= 0) & (row < rows) & (col >= 0) & (col < cols)

    places = (
        north,
        south,
        west.at[1],
        east.at[1],
        west.at[0],
        east.at[0],
        west.at[2],
        east.at[2],
    )
    for d in range(8):

        @pl.when(jnp.logical_not(present(d)))
        def _(d=d):
            places[d][...] = jnp.zeros(places[d].shape, BF16)

    rays = positions_ref.shape[2]
    cell_shape = (TILE // 16, 16, rays)
    cells = (
        lax.broadcasted_iota(jnp.int32, cell_shape, 0) * 16
        + lax.broadcasted_iota(jnp.int32, cell_shape, 1)
    ).astype(F32)
    cells = cells.astype(BF16)
    received[mine] = outgoing[me]
    total[...] = jnp.zeros((TILE, TILE), F32)

    def take(i, unused):
        sources = [partner(TOGETHER * i + j) for j in range(TOGETHER)]
        for source in sources:

            @pl.when(source != mine)
            def _(source=source):
                message(source, here).wait_recv()

        partial = total[...]
        for source in sources:
            partial = deposit_group(received[source], cells, partial)
        total[...] = partial
        return unused

    lax.fori_loop(0, tiles // TOGETHER, take, 0)

    tile = total[...].astype(BF16)
    tile_ref[...] = tile
    exact = tile.astype(F32)
    quarter = lax.div(lax.broadcasted_iota(jnp.int32, (HALO, TILE), 1), HALO)

    def by_quarter(parts):
        return jnp.where(
            quarter < 2,
            jnp.where(quarter == 0, parts[0], parts[1]),
            jnp.where(quarter == 2, parts[2], parts[3]),
        )

    def turn(x, quarters):
        return pltpu.roll(x, quarters % 4 * HALO, 1) if quarters % 4 else x

    bands = [exact[q * HALO : (q + 1) * HALO] for q in range(4)]
    heads[...] = by_quarter([turn(bands[q], q) for q in range(4)]).astype(BF16)
    tails[...] = by_quarter([turn(bands[q], q - 3) for q in range(4)]).astype(BF16)

    first, last = slice(0, HALO), slice(TILE - HALO, TILE)
    parts = (
        (tile_ref.at[first], south),
        (tile_ref.at[last], north),
        (heads, east.at[1]),
        (tails, west.at[1]),
        (heads, east.at[2]),
        (tails, west.at[2]),
        (heads, east.at[0]),
        (tails, west.at[0]),
    )
    opposite = (1, 0, 3, 2, 7, 6, 5, 4)

    def halo(d):
        row, col = neighbour(d)
        return pltpu.make_async_remote_copy(
            src_ref=parts[d][0],
            dst_ref=parts[d][1],
            send_sem=halo_send.at[d],
            recv_sem=halo_recv.at[d],
            device_id={"row": row, "col": col},
            device_id_type=MESH,
        )

    for d in (2, 3, 4, 5, 6, 7, 0, 1):

        @pl.when(present(d))
        def _(d=d):
            halo(d).start()

    loads[2].wait()
    build_toeplitz(profile_ref, table, inner, outer)

    def empty(lines):
        return jnp.zeros((lines, TILE), F32)

    def sweep(products):
        def step(i, sums):
            product = products(pl.ds(pl.multiple_of((3 - i) * 2 * TILE, 2 * TILE), 2 * TILE))
            tall = product.shape[0]
            odd = pltpu.roll(product[:, TILE:], tall - 1, 0)
            return pltpu.roll(sums, tall - 2, 0) + product[:, :TILE] + odd

        return lax.fori_loop(0, 4, step, jnp.zeros((TILE + 16, TILE), F32), unroll=True)[:TILE]

    def dot(a, b):
        return jnp.dot(a, b, preferred_element_type=F32)

    shifted[:, :TILE] = jnp.concatenate([empty(HALO), exact, empty(HALO)], axis=0).astype(BF16)
    shifted[:, TILE:] = jnp.concatenate(
        [empty(HALO - 8), exact, empty(HALO + 8)], axis=0
    ).astype(BF16)
    own[...] = sweep(
        lambda columns: sum(
            dot(shifted[16 * v : 16 * v + TILE + 16, :], inner[v, :, columns]) for v in range(4)
        )
    )

    def drain(target, unused):
        @pl.when(target != mine)
        def _():
            message(mine, device(target)).wait_send()

        return unused

    lax.fori_loop(0, tiles, drain, 0)

    for d in range(8):

        @pl.when(present(d))
        def _(d=d):
            halo(d).wait_send()
            halo(opposite[d]).wait_recv()

    tall = TILE + 2 * HALO
    lanes = lax.broadcasted_iota(jnp.int32, (tall, TILE), 1)
    wests = [west[i].astype(F32) for i in range(3)]
    easts = [east[i].astype(F32) for i in range(3)]

    def band(i, q):
        return by_quarter(
            [turn(wests[i], -q), turn(easts[i], 1 - q), turn(wests[i], 2 - q), turn(easts[i], 3 - q)]
        )

    side = jnp.concatenate([band(0, 3)] + [band(1, q) for q in range(4)] + [band(2, 0)], axis=0)
    side_later = jnp.concatenate([side[8:], empty(8)], axis=0)
    sides = jnp.where(lanes < 2 * HALO, side, side_later).astype(BF16)
    beside[:, :TILE] = sides[: tall - 16]
    beside[:, TILE:] = sides[16:]
    above = north[...].astype(F32)
    below = south[...].astype(F32)
    before = jnp.concatenate(
        [above, jnp.concatenate([above[8:], empty(8)], axis=0)], axis=1
    ).astype(BF16)
    after = jnp.concatenate(
        [jnp.concatenate([empty(8), below[:-8]], axis=0), below], axis=1
    ).astype(BF16)

    def around(columns):
        wide = sum(
            dot(beside[32 * v : 32 * v + TILE + 16, :], outer[v, :, columns]) for v in range(2)
        )
        upper = dot(before, inner[0, :, columns])
        upper_next = dot(before[16:], inner[1, :, columns])
        lower = dot(after, inner[3, :, columns])
        lower_next = dot(after[:16], inner[2, :, columns])
        end = TILE + 8 - HALO
        return jnp.concatenate(
            [
                wide[:16] + upper[:16] + upper_next,
                wide[16:HALO] + upper[16:],
                wide[HALO:end],
                wide[end : end + 16] + lower[:16],
                wide[end + 16 : end + 32] + lower[16:] + lower_next,
                wide[end + 32 :],
            ],
            axis=0,
        )

    edge = table[DISC - 1 : DISC, TILE - HALO : TILE - HALO + 1]
    result = own[...] + jnp.concatenate([exact[HALO:], below], axis=0) * edge + sweep(around)
    out_ref[...] = result * (1.0 / density)


def shards(positions, destination, profile):
    rows = lax.axis_size("row")
    cols = lax.axis_size("col")
    tiles = rows * cols
    blocks, _, rays = positions.shape
    density = blocks * rays / (TILE * TILE)
    tall = TILE + 2 * HALO
    vmem = pl.BlockSpec(memory_space=pltpu.VMEM)
    return pl.pallas_call(
        functools.partial(body, rows, cols, density),
        out_shape=pltpu.VMEM((TILE, TILE), F32),
        in_specs=[pl.BlockSpec(memory_space=pltpu.HBM)] * 3,
        out_specs=vmem,
        scratch_shapes=[
            pltpu.VMEM((blocks, 2, rays), F32),
            pltpu.VMEM((1, blocks), jnp.int32),
            pltpu.VMEM((DISC, DISC), F32),
            pltpu.VMEM((tiles, GROUP, 2 * rays // 3), jnp.int32),
            pltpu.VMEM((tiles, GROUP, 2 * rays // 3), jnp.int32),
            pltpu.VMEM((72, TILE), F32),
            pltpu.VMEM((4, 2 * TILE, 8 * TILE), BF16),
            pltpu.VMEM((2, 2 * TILE, 8 * TILE), BF16),
            pltpu.VMEM((TILE, TILE), BF16),
            pltpu.VMEM((HALO, TILE), BF16),
            pltpu.VMEM((HALO, TILE), BF16),
            pltpu.VMEM((3, HALO, TILE), BF16),
            pltpu.VMEM((3, HALO, TILE), BF16),
            pltpu.VMEM((HALO, TILE), BF16),
            pltpu.VMEM((HALO, TILE), BF16),
            pltpu.VMEM((tall, 2 * TILE), BF16),
            pltpu.VMEM((tall - 16, 2 * TILE), BF16),
            pltpu.VMEM((TILE, TILE), F32),
            pltpu.VMEM((TILE, TILE), F32),
            pltpu.SemaphoreType.DMA((tiles,)),
            pltpu.SemaphoreType.DMA((tiles,)),
            pltpu.SemaphoreType.REGULAR((cols,)),
            pltpu.SemaphoreType.DMA((8,)),
            pltpu.SemaphoreType.DMA((8,)),
            pltpu.SemaphoreType.DMA((3,)),
        ],
        compiler_params=pltpu.CompilerParams(
            collective_id=0, has_side_effects=True
        ),
        name="lens_map",
    )(positions, destination.reshape(1, blocks), profile)


def solution(mesh):
    placed = (P(("maps", "row", "col"), None, None), P(("maps", "row", "col"), None), P())
    return jax.shard_map(
        shards, mesh=mesh, in_specs=placed, out_specs=P(("maps", "row"), "col"), check_vma=False
    )
```

```python
import functools

import jax
import jax.numpy as jnp
from jax import lax
from jax.experimental import pallas as pl
from jax.experimental.pallas import tpu as pltpu
from jax.sharding import PartitionSpec as P

TILE = 128
HALO = 32
MOST = 4
DISC = 2 * HALO + 1
GROUP = 2 * MOST
TOGETHER = 8
FRACTION = 14
BITS = 21
BF16 = jnp.bfloat16
F32 = jnp.float32
MESH = pl.DeviceIdType.MESH
SIDES = ((-1, 0), (1, 0), (0, -1), (0, 1), (-1, -1), (-1, 1), (1, -1), (1, 1))


def code(coords):
    scaled = coords * float(1 << FRACTION)
    whole = jnp.floor(scaled)
    fixed = whole.astype(jnp.int32)
    return jnp.where(scaled > whole, fixed | 1, fixed) + 1


def sevens(x):
    return [((x >> shift) & 127).astype(F32).astype(BF16) for shift in (0, 7, 14)]


def choose(destination_ref, tiles):
    blocks = destination_ref.shape[1]
    wide = 6 * blocks
    targets = jnp.concatenate([destination_ref[...]] * 6, axis=1)
    lane = lax.broadcasted_iota(jnp.int32, (1, wide), 1)
    piece = sum((lane >= i * blocks).astype(jnp.int32) for i in range(1, 6))
    onehot = jnp.where(lax.broadcasted_iota(jnp.int32, (tiles, wide), 0) == targets, 1.0, 0.0)
    earlier = jnp.where(
        lax.broadcasted_iota(jnp.int32, (blocks, wide), 0) < lane - piece * blocks, 1.0, 0.0
    )
    before = jnp.dot(
        onehot[:, :blocks].astype(BF16), earlier.astype(BF16), preferred_element_type=F32
    )
    rank = jnp.sum(before * onehot, axis=0, keepdims=True).astype(jnp.int32)
    second = piece >= 3
    slot = targets * GROUP + rank + jnp.where(second, MOST, 0)
    order = jnp.where(second, piece - 3, piece)
    weight = jnp.where(order == 0, 1.0, jnp.where(order == 1, 128.0, 16384.0))
    rows = lax.broadcasted_iota(jnp.int32, (tiles * GROUP, wide), 0)
    return jnp.where(rows == slot, weight, 0.0).astype(BF16)


def pack(positions_ref, chosen, outgoing):
    tiles = outgoing.shape[0]
    third = outgoing.shape[2] // 2
    pieces = [piece for c in range(2) for piece in sevens(code(positions_ref[:, c, :]))]
    picked = jnp.dot(chosen, jnp.concatenate(pieces, axis=0), preferred_element_type=F32)
    picked = picked.astype(jnp.int32).reshape(tiles, GROUP, 3 * third)
    low, high, cut = (picked[:, :, i * third : (i + 1) * third] for i in range(3))
    outgoing[:, :, :third] = low | (cut << BITS)
    outgoing[:, :, third:] = high | ((cut >> (32 - BITS)) << BITS)


def unpack(words):
    third = words.shape[1] // 2
    one, two = words[:, :third], words[:, third:]
    mask = (1 << BITS) - 1
    cut = lax.shift_right_logical(one, BITS) | (lax.shift_right_logical(two, BITS) << (32 - BITS))
    return jnp.concatenate([one & mask, two & mask, cut], axis=1)


def build_toeplitz(profile_ref, table, inner, outer):
    table[...] = jnp.zeros_like(table)
    weights = profile_ref[...]
    down = lax.broadcasted_iota(jnp.int32, weights.shape, 0) - HALO
    across = lax.broadcasted_iota(jnp.int32, weights.shape, 1) - HALO
    weights = jnp.where(down * down + across * across <= HALO * HALO, weights, 0.0)
    total = jnp.sum(jnp.sum(weights, axis=1, keepdims=True), axis=0, keepdims=True)
    table[0:DISC, 0:DISC] = weights / total
    square = (TILE, TILE)
    row = lax.broadcasted_iota(jnp.int32, square, 0)
    column = lax.broadcasted_iota(jnp.int32, square, 1)
    flip = jnp.where((row + column) % TILE == 0, 1.0, 0.0).astype(BF16)
    table[...] = jnp.dot(table[...].astype(BF16), flip, preferred_element_type=F32)
    core_mask = jnp.abs(row - column) <= HALO
    side_row = row[: 2 * HALO]
    side_mask = jnp.where(side_row < HALO, column[: 2 * HALO], TILE - 1 - column[: 2 * HALO]) < 2 * HALO

    def eight(u, unused):
        v, h = lax.div(u, 2), lax.rem(u, 2)
        lines = table[pl.ds(pl.multiple_of(u * 8, 8), 8), :]
        core = pl.ds(pl.multiple_of(h * TILE, TILE), TILE)
        side = pl.ds(pl.multiple_of(lax.rem(u, 4) * 2 * HALO, 2 * HALO), 2 * HALO)
        for s in range(8):
            line = jnp.broadcast_to(lines[s : s + 1, :], square)
            circulant = pltpu.roll(line, 0, 1, stride=1, stride_axis=0)
            turned = jnp.concatenate([circulant[HALO:], circulant[:HALO]], axis=0)
            columns = slice(s * TILE, (s + 1) * TILE)
            inner[v, core, columns] = jnp.where(core_mask, turned, 0.0).astype(BF16)
            outer[lax.div(u, 4), side, columns] = jnp.where(side_mask, circulant[: 2 * HALO], 0.0).astype(BF16)
        return unused

    lax.fori_loop(0, 8, eight, 0)


def deposit_group(group, cells, total):
    fixed = unpack(group)
    filled = fixed > 0
    fixed = fixed - 1
    part = (fixed & ((1 << FRACTION) - 1)).astype(F32) * (1.0 / (1 << FRACTION))
    low = (fixed >> FRACTION).astype(F32).astype(BF16)
    here = (1.0 - part).astype(BF16)
    there = jnp.where(filled, part, 0.0).astype(BF16)
    rays = fixed.shape[1]
    packed = (1, 16, rays)
    zero = jnp.zeros((), BF16)
    earlier = cells - jnp.ones((), BF16)

    def row(x, k):
        return jnp.broadcast_to(x[k : k + 1, :], packed[1:]).reshape(packed)

    def hat(k):
        base, upper, lower = row(low, k), row(here, k), row(there, k)
        pieces = jnp.where(cells == base, upper, jnp.where(earlier == base, lower, zero))
        return pieces.reshape(TILE, rays)

    first = jnp.concatenate([hat(m) for m in range(MOST)], axis=1)
    second = jnp.concatenate([hat(MOST + m) for m in range(MOST)], axis=1)
    return total + lax.dot_general(
        first, second, (((1,), (1,)), ((), ())), preferred_element_type=F32
    )


def body(
    rows,
    cols,
    density,
    positions_hbm,
    destination_hbm,
    profile_hbm,
    out_ref,
    positions_ref,
    destination_ref,
    profile_ref,
    outgoing,
    received,
    table,
    inner,
    outer,
    tile_ref,
    north,
    south,
    west,
    east,
    heads,
    tails,
    shifted,
    beside,
    own,
    total,
    send_sems,
    recv_sems,
    notices,
    halo_send,
    halo_recv,
    load_sems,
):
    tiles = rows * cols
    my_row = lax.axis_index("row")
    my_col = lax.axis_index("col")
    me = my_row * cols + my_col
    mine = my_col * rows + my_row

    loads = [
        pltpu.make_async_copy(source, target, load_sems.at[i])
        for i, (source, target) in enumerate(
            (
                (destination_hbm, destination_ref),
                (positions_hbm, positions_ref),
                (profile_hbm, profile_ref),
            )
        )
    ]
    for load in loads:
        load.start()

    def message(source, at):
        target = at["col"] * rows + at["row"]
        return pltpu.make_async_remote_copy(
            src_ref=outgoing.at[at["row"] * cols + at["col"]],
            dst_ref=received.at[source],
            send_sem=send_sems.at[target],
            recv_sem=recv_sems.at[source],
            device_id=at,
            device_id_type=MESH,
        )

    here = {"row": my_row, "col": my_col}

    def device(order):
        return {"row": lax.rem(order, rows), "col": lax.div(order, rows)}

    barrier = pltpu.get_barrier_semaphore()

    def greet(target, unused):
        pl.semaphore_signal(barrier, inc=1, device_id=device(target), device_id_type=MESH)
        return unused

    lax.fori_loop(mine + 1, tiles, greet, 0)

    def settle(semaphore, count):
        @pl.when(count > 0)
        def _():
            pl.semaphore_wait(semaphore, count)

    settle(barrier, mine)

    def tell(at):
        pl.semaphore_signal(notices.at[my_col], inc=1, device_id=at, device_id_type=MESH)

    def lower(act, near_first=False):
        def column(col, unused):
            for row in reversed(range(rows)):
                act({"row": row, "col": col})
            return unused

        def inside(row, unused):
            act({"row": row, "col": my_col})
            return unused

        if near_first:
            lax.fori_loop(0, my_row, inside, 0)
        lax.fori_loop(0, my_col, column, 0)
        if not near_first:
            lax.fori_loop(0, my_row, inside, 0)

    lower(tell, True)
    loads[0].wait()
    chosen = choose(destination_ref, tiles)
    loads[1].wait()
    pack(positions_ref, chosen, outgoing)

    def start(at):
        message(mine, at).start()

    lower(start)

    def send_up(col, unused):
        first = jnp.where(col == my_col, my_row + 1, 0)
        settle(notices.at[col], rows - first)

        def each(row, done):
            start({"row": row, "col": col})
            return done

        lax.fori_loop(first, rows, each, 0)

        return unused

    lax.fori_loop(my_col, cols, send_up, 0)
    near = rows * (2 if cols % 2 == 0 else 1)
    base = lax.div(mine, near) * near
    ceiling = base + near

    def partner(j):
        ahead = mine + j
        within = jnp.where(ahead >= ceiling, ahead - near, ahead)
        rest = j - near
        return jnp.where(j < near, within, jnp.where(rest < base, base - 1 - rest, j))

    def neighbour(d):
        down, right = SIDES[d]
        return my_row + down, my_col + right

    def present(d):
        row, col = neighbour(d)
        return (row >= 0) & (row < rows) & (col >= 0) & (col < cols)

    places = (
        north,
        south,
        west.at[1],
        east.at[1],
        west.at[0],
        east.at[0],
        west.at[2],
        east.at[2],
    )
    for d in range(8):

        @pl.when(jnp.logical_not(present(d)))
        def _(d=d):
            places[d][...] = jnp.zeros(places[d].shape, BF16)

    rays = positions_ref.shape[2]
    cell_shape = (TILE // 16, 16, rays)
    cells = (
        lax.broadcasted_iota(jnp.int32, cell_shape, 0) * 16
        + lax.broadcasted_iota(jnp.int32, cell_shape, 1)
    ).astype(F32)
    cells = cells.astype(BF16)
    received[mine] = outgoing[me]
    total[...] = jnp.zeros((TILE, TILE), F32)

    def take(i, unused):
        sources = [partner(TOGETHER * i + j) for j in range(TOGETHER)]
        for source in sources:

            @pl.when(source != mine)
            def _(source=source):
                message(source, here).wait_recv()

        partial = total[...]
        for source in sources:
            partial = deposit_group(received[source], cells, partial)
        total[...] = partial
        return unused

    lax.fori_loop(0, tiles // TOGETHER, take, 0)

    tile = total[...].astype(BF16)
    tile_ref[...] = tile
    exact = tile.astype(F32)
    quarter = lax.div(lax.broadcasted_iota(jnp.int32, (HALO, TILE), 1), HALO)

    def by_quarter(parts):
        return jnp.where(
            quarter < 2,
            jnp.where(quarter == 0, parts[0], parts[1]),
            jnp.where(quarter == 2, parts[2], parts[3]),
        )

    def turn(x, quarters):
        return pltpu.roll(x, quarters % 4 * HALO, 1) if quarters % 4 else x

    bands = [exact[q * HALO : (q + 1) * HALO] for q in range(4)]
    heads[...] = by_quarter([turn(bands[q], q) for q in range(4)]).astype(BF16)
    tails[...] = by_quarter([turn(bands[q], q - 3) for q in range(4)]).astype(BF16)

    first, last = slice(0, HALO), slice(TILE - HALO, TILE)
    parts = (
        (tile_ref.at[first], south),
        (tile_ref.at[last], north),
        (heads, east.at[1]),
        (tails, west.at[1]),
        (heads, east.at[2]),
        (tails, west.at[2]),
        (heads, east.at[0]),
        (tails, west.at[0]),
    )
    opposite = (1, 0, 3, 2, 7, 6, 5, 4)

    def halo(d):
        row, col = neighbour(d)
        return pltpu.make_async_remote_copy(
            src_ref=parts[d][0],
            dst_ref=parts[d][1],
            send_sem=halo_send.at[d],
            recv_sem=halo_recv.at[d],
            device_id={"row": row, "col": col},
            device_id_type=MESH,
        )

    for d in (2, 3, 4, 5, 6, 7, 0, 1):

        @pl.when(present(d))
        def _(d=d):
            halo(d).start()

    loads[2].wait()
    build_toeplitz(profile_ref, table, inner, outer)

    def empty(lines):
        return jnp.zeros((lines, TILE), F32)

    def sweep(products):
        def step(i, sums):
            product = products(pl.ds(pl.multiple_of((3 - i) * 2 * TILE, 2 * TILE), 2 * TILE))
            tall = product.shape[0]
            odd = pltpu.roll(product[:, TILE:], tall - 1, 0)
            return pltpu.roll(sums, tall - 2, 0) + product[:, :TILE] + odd

        return lax.fori_loop(0, 4, step, jnp.zeros((TILE + 16, TILE), F32), unroll=True)[:TILE]

    def dot(a, b):
        return jnp.dot(a, b, preferred_element_type=F32)

    shifted[:, :TILE] = jnp.concatenate([empty(HALO), exact, empty(HALO)], axis=0).astype(BF16)
    shifted[:, TILE:] = jnp.concatenate(
        [empty(HALO - 8), exact, empty(HALO + 8)], axis=0
    ).astype(BF16)
    own[...] = sweep(
        lambda columns: sum(
            dot(shifted[16 * v : 16 * v + TILE + 16, :], inner[v, :, columns]) for v in range(4)
        )
    )

    def drain(target, unused):
        @pl.when(target != mine)
        def _():
            message(mine, device(target)).wait_send()

        return unused

    lax.fori_loop(0, tiles, drain, 0)

    for d in range(8):

        @pl.when(present(d))
        def _(d=d):
            halo(d).wait_send()
            halo(opposite[d]).wait_recv()

    tall = TILE + 2 * HALO
    lanes = lax.broadcasted_iota(jnp.int32, (tall, TILE), 1)
    wests = [west[i].astype(F32) for i in range(3)]
    easts = [east[i].astype(F32) for i in range(3)]

    def band(i, q):
        return by_quarter(
            [turn(wests[i], -q), turn(easts[i], 1 - q), turn(wests[i], 2 - q), turn(easts[i], 3 - q)]
        )

    side = jnp.concatenate([band(0, 3)] + [band(1, q) for q in range(4)] + [band(2, 0)], axis=0)
    side_later = jnp.concatenate([side[8:], empty(8)], axis=0)
    sides = jnp.where(lanes < 2 * HALO, side, side_later).astype(BF16)
    beside[:, :TILE] = sides[: tall - 16]
    beside[:, TILE:] = sides[16:]
    above = north[...].astype(F32)
    below = south[...].astype(F32)
    before = jnp.concatenate(
        [above, jnp.concatenate([above[8:], empty(8)], axis=0)], axis=1
    ).astype(BF16)
    after = jnp.concatenate(
        [jnp.concatenate([empty(8), below[:-8]], axis=0), below], axis=1
    ).astype(BF16)

    def around(columns):
        wide = sum(
            dot(beside[32 * v : 32 * v + TILE + 16, :], outer[v, :, columns]) for v in range(2)
        )
        upper = dot(before, inner[0, :, columns])
        upper_next = dot(before[16:], inner[1, :, columns])
        lower = dot(after, inner[3, :, columns])
        lower_next = dot(after[:16], inner[2, :, columns])
        end = TILE + 8 - HALO
        return jnp.concatenate(
            [
                wide[:16] + upper[:16] + upper_next,
                wide[16:HALO] + upper[16:],
                wide[HALO:end],
                wide[end : end + 16] + lower[:16],
                wide[end + 16 : end + 32] + lower[16:] + lower_next,
                wide[end + 32 :],
            ],
            axis=0,
        )

    edge = table[DISC - 1 : DISC, TILE - HALO : TILE - HALO + 1]
    result = own[...] + jnp.concatenate([exact[HALO:], below], axis=0) * edge + sweep(around)
    out_ref[...] = result * (1.0 / density)


def shards(positions, destination, profile):
    rows = lax.axis_size("row")
    cols = lax.axis_size("col")
    tiles = rows * cols
    blocks, _, rays = positions.shape
    density = blocks * rays / (TILE * TILE)
    tall = TILE + 2 * HALO
    vmem = pl.BlockSpec(memory_space=pltpu.VMEM)
    return pl.pallas_call(
        functools.partial(body, rows, cols, density),
        out_shape=pltpu.VMEM((TILE, TILE), F32),
        in_specs=[pl.BlockSpec(memory_space=pltpu.HBM)] * 3,
        out_specs=vmem,
        scratch_shapes=[
            pltpu.VMEM((blocks, 2, rays), F32),
            pltpu.VMEM((1, blocks), jnp.int32),
            pltpu.VMEM((DISC, DISC), F32),
            pltpu.VMEM((tiles, GROUP, 2 * rays // 3), jnp.int32),
            pltpu.VMEM((tiles, GROUP, 2 * rays // 3), jnp.int32),
            pltpu.VMEM((72, TILE), F32),
            pltpu.VMEM((4, 2 * TILE, 8 * TILE), BF16),
            pltpu.VMEM((2, 2 * TILE, 8 * TILE), BF16),
            pltpu.VMEM((TILE, TILE), BF16),
            pltpu.VMEM((HALO, TILE), BF16),
            pltpu.VMEM((HALO, TILE), BF16),
            pltpu.VMEM((3, HALO, TILE), BF16),
            pltpu.VMEM((3, HALO, TILE), BF16),
            pltpu.VMEM((HALO, TILE), BF16),
            pltpu.VMEM((HALO, TILE), BF16),
            pltpu.VMEM((tall, 2 * TILE), BF16),
            pltpu.VMEM((tall - 16, 2 * TILE), BF16),
            pltpu.VMEM((TILE, TILE), F32),
            pltpu.VMEM((TILE, TILE), F32),
            pltpu.SemaphoreType.DMA((tiles,)),
            pltpu.SemaphoreType.DMA((tiles,)),
            pltpu.SemaphoreType.REGULAR((cols,)),
            pltpu.SemaphoreType.DMA((8,)),
            pltpu.SemaphoreType.DMA((8,)),
            pltpu.SemaphoreType.DMA((3,)),
        ],
        compiler_params=pltpu.CompilerParams(
            collective_id=0, has_side_effects=True
        ),
        name="lens_map",
    )(positions, destination.reshape(1, blocks), profile)


def solution(mesh):
    placed = (P(("maps", "row", "col"), None, None), P(("maps", "row", "col"), None), P())
    return jax.shard_map(
        shards, mesh=mesh, in_specs=placed, out_specs=P(("maps", "row"), "col"), check_vma=False
    )
```
